256 devices in a mesh: gx: 16 (over z, core), gy: 4 (over x), gz: 4 (over y).
Axes of the slice: x: 4, y: 4, z: 8, core: 2. Of those that a mesh axis runs over, the one named last changes fastest.
Arguments:
- velocity: float32 [3, 1024, 64, 512], P(None, 'gx', 'gy', 'gz'), may hold values from -6 to 6
- viscosity: float32 [1024, 64, 512], P('gx', 'gy', 'gz'), may hold values from 0.01 to 0.3
- point_force: float32 [3, 262144], P(None, ('gx', 'gy', 'gz')), may hold values from -300 to 300
- point_offset: float32 [3, 262144], P(None, ('gx', 'gy', 'gz')), may hold values from 0 to 1
- point_cell: int32 [262144], P(('gx', 'gy', 'gz')), may hold values from 0 to 131071, as said below
- point_tile: int32 [262144, 1], P(('gx', 'gy', 'gz')), may hold values from 0 to 255, as said below
Outputs:
- new_velocity: float32 [3, 1024, 64, 512], P(None, 'gx', 'gy', 'gz')
- point_velocity: float32 [3, 262144], P(None, ('gx', 'gy', 'gz'))
The draws below stay inside these ranges and needn't reach their ends.
Inputs may be any that keep to these rules, and one draw needn't show every extreme that they name: `point_tile`: the 1024 points of one device form 8 runs of 128 points in a row; each run names one tile, the 8 tiles of a device differ, the first is the device's own tile and the others differ from it by at most one in each of the three tile coordinates. `point_cell`: the cell's flat index (i * 16 + j) * 128 + k within its tile.
All inputs are finite; a program needn't handle non-finite values.
Results may differ from the reference program's by a relative error of at most 0.0003.
Values sent between devices are 32-bit elements; how exact they have to be, the bound alone decides.
No kernel may reach another device: no remote copies, remote signals or barrier semaphores. Data moves between devices by JAX's collectives and lax.ppermute only.
A program may use at most 64 MiB of HBM per device.

```python
import math
import jax
import jax.numpy as jnp
from jax import lax

CX = 64
CY = 16
CZ = 128
PTS_DEV = 1024
NX = 1024
NY = 64
NZ = 512
POINTS = 262144
CAP = 128
SLOTS = 3456
N_GX = 16
N_GY = 4
N_GZ = 4


def draw_point_tile(key, part):
    devices = N_GX * N_GY * N_GZ
    source = jnp.arange(devices, dtype=jnp.int32)
    source_a = source // (N_GY * N_GZ)
    source_b = source // N_GZ % N_GY
    source_c = source % N_GZ
    beside_all = jnp.arange(27, dtype=jnp.int32)
    step_a = beside_all // 9 - 1
    step_b = beside_all // 3 % 3 - 1
    step_c = beside_all % 3 - 1
    target_a = source_a[:, None] + step_a[None, :]
    target_b = source_b[:, None] + step_b[None, :]
    target_c = source_c[:, None] + step_c[None, :]
    inside = (target_a >= 0) & (target_a < N_GX) & (target_b >= 0) & (target_b < N_GY) & (target_c >= 0) & (target_c < N_GZ)
    scores = jax.random.randint(jax.random.fold_in(key, 11), (devices, 27), 0, 1 << 20) * 32 + beside_all[None, :]
    scores = jnp.where(inside, scores, -1)
    scores = jnp.where(beside_all[None, :] == 13, 1 << 30, scores)
    _, chosen = lax.top_k(scores, 8)
    target_tile = (target_a * N_GY + target_b) * N_GZ + target_c
    picked = jnp.take_along_axis(target_tile, chosen, axis=1)
    run_of_point = jnp.arange(PTS_DEV, dtype=jnp.int32) // CAP
    tiles = picked[:, run_of_point]
    return tiles.reshape(POINTS, 1).astype(jnp.int32)


def draw_point_cell(key, part):
    runs = POINTS // CAP
    start_i = jax.random.randint(jax.random.fold_in(key, 21), (runs,), 0, CX)
    start_j = jax.random.randint(jax.random.fold_in(key, 22), (runs,), 0, CY)
    start_k = jax.random.randint(jax.random.fold_in(key, 23), (runs,), 0, CZ)
    start_i = start_i.at[0].set(CX - 1).at[1].set(0)
    start_j = start_j.at[0].set(CY - 1).at[1].set(0)
    start_k = start_k.at[0].set(CZ - 1).at[1].set(0)
    turn_i = jax.random.randint(jax.random.fold_in(key, 24), (runs,), -1, 2)
    turn_j = jax.random.randint(jax.random.fold_in(key, 25), (runs,), -1, 2)
    turn_k = jax.random.randint(jax.random.fold_in(key, 26), (runs,), 0, 2) * 2 - 1
    along = jnp.arange(CAP, dtype=jnp.int32)
    cell_i = jnp.clip(start_i[:, None] + turn_i[:, None] * (along * CX // (2 * CAP))[None, :], 0, CX - 1)
    cell_j = jnp.clip(start_j[:, None] + turn_j[:, None] * (along * CY // (2 * CAP))[None, :], 0, CY - 1)
    cell_k = jnp.clip(start_k[:, None] + turn_k[:, None] * (along * CZ // (2 * CAP))[None, :], 0, CZ - 1)
    codes = (cell_i * CY + cell_j) * CZ + cell_k
    return codes.reshape(POINTS).astype(jnp.int32)


def shard_levels(stream_key, shape, split, low, largest):
    loudness, own = 1.0, jax.random.fold_in(stream_key, 6)
    for dim, parts in split:
        draws = jnp.exp(jax.random.uniform(jax.random.fold_in(own, dim), (parts,), jnp.float32, low / len(split), largest / len(split)))
        loudness = loudness * jnp.repeat(draws, shape[dim] // parts).reshape([-1 if axis == dim else 1 for axis in range(len(shape))])
    return loudness


def scatter_about(key, dims, width, reach, pieces=(), kind=jnp.bfloat16):
    values = width * jax.random.normal(key, dims, jnp.float32)
    if pieces:
        values = values * shard_levels(key, dims, pieces, -0.22, 0.18)
    return jnp.clip(values, -reach, reach).astype(kind)


def setup_inputs(seed: int = 0) -> dict:
    key_of = jax.random.split(jax.random.key(seed), 7)
    velocity = scatter_about(key_of[0], (3, NX, NY, NZ), 1.0, 6.0, ((1, 16), (2, 4), (3, 4)), jnp.float32)
    viscosity = jnp.clip(jnp.exp(math.log(0.3) - 3.4011974 * jax.random.uniform(key_of[1], (NX, NY, NZ), jnp.float32) ** shard_levels(key_of[1], (NX, NY, NZ), ((0, 16), (1, 4), (2, 4)), -0.2, 0.2)), 0.01, 0.3)
    point_force = scatter_about(key_of[2], (3, POINTS), 50.0, 300.0, ((1, 256),), jnp.float32)
    point_offset = jnp.clip(1.0 * jax.random.uniform(key_of[3], (3, POINTS), jnp.float32) ** shard_levels(key_of[3], (3, POINTS), ((1, 256),), -0.2, 0.2), 0.0, 1.0)
    point_cell = draw_point_cell(jax.random.fold_in(key_of[6], 71), 0)
    point_tile = draw_point_tile(jax.random.fold_in(key_of[6], 71), 0)
    return {"velocity": velocity, "viscosity": viscosity, "point_force": point_force, "point_offset": point_offset, "point_cell": point_cell, "point_tile": point_tile}


time_step = 0.1
kernel_width = 2.0
one_third = 1.0 / 3.0
two_thirds = 2.0 / 3.0


def bucket_slots(targets):
    point_order = jnp.arange(targets.shape[0], dtype=jnp.int32)
    earlier = (targets[None, :] == targets[:, None]) & (point_order[None, :] < point_order[:, None])
    return jnp.sum(earlier.astype(jnp.int32), axis=1).astype(jnp.int32)


def axis_weights(centre, cell_count):
    middles = jnp.arange(cell_count, dtype=jnp.float32) + 0.5
    scaled = (middles[None, :] - centre[:, None]) / kernel_width
    unscaled = jnp.exp(-scaled * scaled)
    return unscaled / jnp.sum(unscaled, axis=1, keepdims=True)


def point_kernels(cell_codes, offsets, first_cells, second_cells, third_cells):
    plane_cells = second_cells * third_cells
    first_index = cell_codes // plane_cells
    second_index = (cell_codes // third_cells) % second_cells
    third_index = cell_codes % third_cells
    stream_weights = axis_weights(first_index.astype(jnp.float32) + offsets[0], first_cells)
    span_weights = axis_weights(second_index.astype(jnp.float32) + offsets[1], second_cells)
    height_weights = axis_weights(third_index.astype(jnp.float32) + offsets[2], third_cells)
    plane_weights = (span_weights[:, :, None] * height_weights[:, None, :]).reshape(cell_codes.shape[0], plane_cells)
    return stream_weights, plane_weights


def spread_tile(slot_force, slot_offset, slot_cell, first_cells, second_cells, third_cells, block_size):
    slot_count = slot_force.shape[1]

    def one_block(accumulated, block_index):
        first_row = block_index * block_size
        force_block = lax.dynamic_slice_in_dim(slot_force, first_row, block_size, 1)
        offset_block = lax.dynamic_slice_in_dim(slot_offset, first_row, block_size, 1)
        code_block = lax.dynamic_slice_in_dim(slot_cell, first_row, block_size, 0)
        stream_weights, plane_weights = point_kernels(code_block, offset_block, first_cells, second_cells, third_cells)
        weighted = force_block[:, :, None] * stream_weights[None, :, :]
        accumulated = accumulated + jnp.einsum("cqi,qm->cim", weighted, plane_weights, precision=lax.Precision.HIGHEST)
        return accumulated, None

    start_value = jnp.zeros((3, first_cells, second_cells * third_cells), jnp.float32)
    accumulated, _ = lax.scan(one_block, start_value, jnp.arange(slot_count // block_size, dtype=jnp.int32))
    return accumulated.reshape(3, first_cells, second_cells, third_cells)


def sample_tile(field, slot_offset, slot_cell, block_size):
    first_cells, second_cells, third_cells = field.shape[1], field.shape[2], field.shape[3]
    flat_field = field.reshape(3, first_cells, second_cells * third_cells)
    slot_count = slot_cell.shape[0]

    def one_block(carried, block_index):
        first_row = block_index * block_size
        offset_block = lax.dynamic_slice_in_dim(slot_offset, first_row, block_size, 1)
        code_block = lax.dynamic_slice_in_dim(slot_cell, first_row, block_size, 0)
        stream_weights, plane_weights = point_kernels(code_block, offset_block, first_cells, second_cells, third_cells)
        partial_sums = jnp.einsum("cim,qm->ciq", flat_field, plane_weights, precision=lax.Precision.HIGHEST)
        sampled = jnp.sum(partial_sums * stream_weights.T[None, :, :], axis=1)
        return carried, sampled

    _, sampled_blocks = lax.scan(one_block, None, jnp.arange(slot_count // block_size, dtype=jnp.int32))
    return sampled_blocks.transpose(1, 0, 2).reshape(3, slot_count)


def shifted(padded, dimension, distance):
    limits = [slice(None), slice(2, padded.shape[1] - 2), slice(2, padded.shape[2] - 2), slice(2, padded.shape[3] - 2)]
    limits[dimension] = slice(2 + distance, padded.shape[dimension] - 2 + distance)
    return padded[tuple(limits)]


def tendency(padded, viscosity, forcing):
    centre = shifted(padded, 1, 0)
    advection = jnp.zeros_like(centre)
    diffusion = -6.0 * centre
    for dimension in (1, 2, 3):
        ahead_one = shifted(padded, dimension, 1)
        behind_one = shifted(padded, dimension, -1)
        ahead_two = shifted(padded, dimension, 2)
        behind_two = shifted(padded, dimension, -2)
        gradient = (8.0 * (ahead_one - behind_one) - (ahead_two - behind_two)) / 12.0
        advection = advection + centre[dimension - 1][None] * gradient
        diffusion = diffusion + ahead_one + behind_one
    return viscosity[None] * diffusion - advection + forcing


def with_zeros(field):
    return jnp.pad(field, ((0, 0), (2, 2), (2, 2), (2, 2)))


def to_tiles(field):
    devices = N_GX * N_GY * N_GZ
    blocks = field.reshape(3, N_GX, CX, N_GY, CY, N_GZ, CZ).transpose(1, 3, 5, 0, 2, 4, 6)
    return blocks.reshape(devices, 3, CX, CY, CZ)


def from_tiles(tiles):
    blocks = tiles.reshape(N_GX, N_GY, N_GZ, 3, CX, CY, CZ).transpose(3, 0, 4, 1, 5, 2, 6)
    return blocks.reshape(3, NX, NY, NZ)


def tile_coordinates(tile):
    return tile // (N_GY * N_GZ), (tile // N_GZ) % N_GY, tile % N_GZ


def reference(velocity, viscosity, point_force, point_offset, point_cell, point_tile):
    devices = N_GX * N_GY * N_GZ
    targets = point_tile[:, 0].astype(jnp.int32)
    slot_rank = jax.vmap(bucket_slots)(targets.reshape(devices, PTS_DEV)).reshape(POINTS)
    source = jnp.arange(POINTS, dtype=jnp.int32) // PTS_DEV
    source_a, source_b, source_c = tile_coordinates(source)
    target_a, target_b, target_c = tile_coordinates(targets)
    neighbour = ((source_a - target_a + 1) * 3 + source_b - target_b + 1) * 3 + source_c - target_c + 1
    position = (neighbour * CAP + slot_rank).astype(jnp.int32)
    slot_force = jnp.zeros((devices, SLOTS, 3), jnp.float32).at[targets, position].set(point_force.T)
    slot_offset = jnp.zeros((devices, SLOTS, 3), jnp.float32).at[targets, position].set(point_offset.T)
    slot_force = slot_force.transpose(0, 2, 1)
    slot_offset = slot_offset.transpose(0, 2, 1)
    slot_cell = jnp.zeros((devices, SLOTS), jnp.int32).at[targets, position].set(point_cell)
    block_size = 3 * CAP
    tiles = lax.map(lambda members: spread_tile(members[0], members[1], members[2], CX, CY, CZ, block_size), (slot_force, slot_offset, slot_cell))
    forcing = from_tiles(tiles)
    section_one = velocity + time_step * tendency(with_zeros(velocity), viscosity, forcing)
    section_two = 0.75 * velocity + 0.25 * (section_one + time_step * tendency(with_zeros(section_one), viscosity, forcing))
    new_velocity = one_third * velocity + two_thirds * (section_two + time_step * tendency(with_zeros(section_two), viscosity, forcing))
    sampled = lax.map(lambda members: sample_tile(members[0], members[1], members[2], block_size), (to_tiles(new_velocity), slot_offset, slot_cell))
    point_velocity = sampled[targets, :, position].T
    return new_velocity, point_velocity
```

```python
import functools

import jax
import jax.numpy as jnp
from jax import lax
from jax.experimental import pallas as pl
from jax.experimental.pallas import tpu as pltpu
from jax.sharding import PartitionSpec as P

DT = 0.1
CI, CJ, CK = 64, 16, 128
NS = 3 * CI
CAP = 128
RUNS = 8
NY_DEV, NZ_DEV = 4, 4
PAD_ROWS = 32
F32 = jnp.float32
BF16 = jnp.bfloat16


def vmem():
    return pl.BlockSpec(memory_space=pltpu.VMEM)


def smem():
    return pl.BlockSpec(memory_space=pltpu.SMEM)


def shape(*dims):
    return jax.ShapeDtypeStruct(dims, F32)


def params():
    return pltpu.CompilerParams(vmem_limit_bytes=40 * 1024 * 1024)


def run_code(tile_ref, run):
    target = tile_ref[run * CAP]
    step_a = target // (NY_DEV * NZ_DEV) - lax.axis_index("gx")
    step_b = (target // NZ_DEV) % NY_DEV - lax.axis_index("gy")
    step_c = target % NZ_DEV - lax.axis_index("gz")
    return ((step_a + 1) * 3 + step_b + 1) * 3 + step_c + 1


def pack_y(rows_ref, forward_ref, backward_ref):
    for r in range(2):
        for s in range(0, NS, 8):
            forward_ref[r * NS + s : r * NS + s + 8, :] = rows_ref[
                pl.ds(s * CJ + CJ - 2 + r, 8, stride=CJ), :
            ]
            backward_ref[r * NS + s : r * NS + s + 8, :] = rows_ref[
                pl.ds(s * CJ + r, 8, stride=CJ), :
            ]


def pack_x(rows_ref, forward_ref, backward_ref):
    for c in range(3):
        first = c * CI * CJ
        forward_ref[c * 2 * CJ : (c + 1) * 2 * CJ, :] = rows_ref[
            first + (CI - 2) * CJ : first + CI * CJ, :
        ]
        backward_ref[c * 2 * CJ : (c + 1) * 2 * CJ, :] = rows_ref[first : first + 2 * CJ, :]


def z_masks():
    lane = lax.broadcasted_iota(jnp.int32, (CJ, CK), 1)
    return lane


def pack_z(rows_ref, out_ref):
    lane = z_masks()
    group = lane // 4

    def step(u, blocks):
        shift = lax.rem(2 + 4 * u, CK)
        fresh = []
        for b in range(6):
            first = pl.multiple_of((b * 32 + u) * CJ, CJ)
            turned = pltpu.roll(rows_ref[pl.ds(first, CJ), :], shift, 1)
            fresh.append(jnp.where(group == u, turned, blocks[b]))
        return tuple(fresh)

    zero = jnp.zeros((CJ, CK), F32)
    blocks = lax.fori_loop(0, 32, step, (zero,) * 6)
    for b in range(6):
        out_ref[b * CJ : (b + 1) * CJ, :] = blocks[b]


def pack_kernel(
    tile_ref, force_ref, offset_ref, cell_ref, rows_ref,
    points_ref, xf_ref, xb_ref, yf_ref, yb_ref, zp_ref,
):
    points_ref[...] = jnp.zeros_like(points_ref)
    for run in range(RUNS):
        code = run_code(tile_ref, run)
        lanes = slice(run * CAP, (run + 1) * CAP)
        block = jnp.concatenate(
            [
                force_ref[:, lanes],
                offset_ref[:, lanes],
                cell_ref[run : run + 1, :].astype(F32),
                jnp.ones((1, CAP), F32),
            ],
            axis=0,
        )
        points_ref[code] = block
    pack_y(rows_ref, yf_ref, yb_ref)
    pack_x(rows_ref, xf_ref, xb_ref)
    pack_z(rows_ref, zp_ref)


def weights_along(centre, count):
    middle = lax.broadcasted_iota(jnp.int32, (count, centre.shape[1]), 0).astype(F32) + 0.5
    scaled = (middle - centre) * 0.5
    raw = jnp.exp(-scaled * scaled)
    return raw * (1.0 / jnp.sum(raw, axis=0, keepdims=True))


def point_weights(block):
    cell = block[6:7, :].astype(jnp.int32)
    first = (cell // (CJ * CK)).astype(F32) + block[3:4, :]
    second = ((cell // CK) % CJ).astype(F32) + block[4:5, :]
    third = (cell % CK).astype(F32) + block[5:6, :]
    return weights_along(first, CI), weights_along(second, CJ), weights_along(third, CK)


def halves(value):
    high = value.astype(BF16)
    return high, (value - high.astype(F32)).astype(BF16)


def gather_slots(zlo_ref, zmid_ref, zhi_ref, slots, order):
    filled = jnp.zeros((1, CAP), jnp.int32)
    for group, ref in enumerate((zlo_ref, zmid_ref, zhi_ref)):
        for t in range(9):
            s = group * 9 + t
            value = ref[t]
            slots[s] = value
            filled = filled + jnp.where(value[7:8, :] > 0.5, 1 << s, 0)
    slots[27] = jnp.zeros((8, CAP), F32)
    mask = jnp.max(filled)
    count = jnp.int32(0)
    for s in range(27):
        order[count] = s
        count = count + ((mask >> s) & 1)
    order[count] = 27
    return count


def pair_block(slots, order, pair):
    return jnp.concatenate([slots[order[2 * pair]], slots[order[2 * pair + 1]]], axis=1)


NT = (((1,), (1,)), ((), ()))
NN = (((1,), (0,)), ((), ()))


def spread(slots, order, count, acc):
    acc[...] = jnp.zeros_like(acc)

    def one_pair(pair, carry):
        block = pair_block(slots, order, pair)
        wx, wy, wz = point_weights(block)
        ah, al = halves(jnp.concatenate([block[c : c + 1, :] * wx for c in range(3)], axis=0))
        for j in range(0, CJ, 2):
            plane = jnp.concatenate([wz * wy[j : j + 1, :], wz * wy[j + 1 : j + 2, :]], axis=0)
            bh, bl = halves(plane)
            total = lax.dot_general(ah, bh, NT, preferred_element_type=F32)
            total = total + lax.dot_general(ah, bl, NT, preferred_element_type=F32)
            total = total + lax.dot_general(al, bh, NT, preferred_element_type=F32)
            acc[:, j * CK : (j + 2) * CK] += total
        return carry

    lax.fori_loop(0, (count + 1) // 2, one_pair, 0)


def edge_flags():
    ax, ay, az = (lax.axis_index(n) for n in ("gx", "gy", "gz"))
    nx, ny, nz = (lax.axis_size(n) for n in ("gx", "gy", "gz"))
    return (
        (ax > 0, ax < nx - 1),
        (ay > 0, ay < ny - 1),
        (az > 0, az < nz - 1),
    )


def stage(alpha, beta, rows_ref, base_ref, visc_ref, forcing_ref, halos, padded, zsc, out_ref):
    xlo, xhi, ylo, yhi, zlo, zhi = halos
    (x0, x1), (y0, y1), (z0, z1) = edge_flags()
    step_rows = (CI + 4) * PAD_ROWS
    for c in range(3):
        for n, (ref, ok) in enumerate(((xlo, x0), (xhi, x1))):
            for r in range(2):
                value = ref[(c * 2 + r) * CJ : (c * 2 + r + 1) * CJ, :]
                first = c * step_rows + (n * (CI + 2) + r) * PAD_ROWS + 8
                padded[first : first + CJ, :] = jnp.where(ok, value, 0.0)
        for i in range(0, CI, 8):
            for n, (ref, ok) in enumerate(((ylo, y0), (yhi, y1))):
                for r in range(2):
                    value = ref[r * NS + c * CI + i : r * NS + c * CI + i + 8, :]
                    first = c * step_rows + (i + 2) * PAD_ROWS + (6 + r if n == 0 else 24 + r)
                    padded[pl.ds(first, 8, stride=PAD_ROWS), :] = jnp.where(ok, value, 0.0)
    lane = z_masks()
    low_part = lane % 4 < 2
    for b in range(6):
        part = slice(b * CJ, (b + 1) * CJ)
        zsc[part, :] = jnp.where(
            low_part, jnp.where(z0, zlo[part, :], 0.0), jnp.where(z1, zhi[part, :], 0.0)
        )

    def fill(i, carry):
        for c in range(3):
            source = pl.multiple_of((c * CI + i) * CJ, CJ)
            target = pl.multiple_of(c * step_rows + (i + 2) * PAD_ROWS + 8, 8)
            padded[pl.ds(target, CJ), :] = rows_ref[pl.ds(source, CJ), :]
        return carry

    lax.fori_loop(0, CI, fill, 0)

    at0, at01 = lane == 0, lane < 2
    at127, at126 = lane == CK - 1, lane >= CK - 2

    def one_plane(i, carry):
        shift = lax.rem(2 * CK - 2 - 4 * lax.rem(i, 32), CK)
        visc = visc_ref[pl.ds(pl.multiple_of(i * CJ, CJ), CJ), :]

        def at(c, di, dj):
            first = c * step_rows + (i + 2 + di) * PAD_ROWS + 8 + dj
            return padded[pl.ds(first, CJ), :]

        centre = [at(c, 0, 0) for c in range(3)]
        for c in range(3):
            here = centre[c]
            block = pl.multiple_of((2 * c + i // 32) * CJ, CJ)
            side = pltpu.roll(zsc[pl.ds(block, CJ), :], shift, 1)
            za1 = pltpu.roll(jnp.where(at0, side, here), CK - 1, 1)
            za2 = pltpu.roll(jnp.where(at01, side, here), CK - 2, 1)
            zb1 = pltpu.roll(jnp.where(at127, side, here), 1, 1)
            zb2 = pltpu.roll(jnp.where(at126, side, here), 2, 1)
            xa1, xb1, xa2, xb2 = at(c, 1, 0), at(c, -1, 0), at(c, 2, 0), at(c, -2, 0)
            ya1, yb1, ya2, yb2 = at(c, 0, 1), at(c, 0, -1), at(c, 0, 2), at(c, 0, -2)
            advect = centre[0] * (8.0 * (xa1 - xb1) - (xa2 - xb2))
            advect = advect + centre[1] * (8.0 * (ya1 - yb1) - (ya2 - yb2))
            advect = advect + centre[2] * (8.0 * (za1 - zb1) - (za2 - zb2))
            diffuse = ((xa1 + xb1) + (ya1 + yb1)) + ((za1 + zb1) - 6.0 * here)
            where = pl.ds(pl.multiple_of((c * CI + i) * CJ, CJ), CJ)
            rate = visc * diffuse - advect * (1.0 / 12.0) + forcing_ref[where, :]
            fresh = beta * (here + DT * rate)
            if alpha:
                fresh = fresh + alpha * base_ref[where, :]
            out_ref[where, :] = fresh
        return carry

    lax.fori_loop(0, CI, one_plane, 0)


def first_kernel(
    zlo_p, zmid_p, zhi_p, rows_ref, visc_ref, xlo, xhi, ylo, yhi, zlo, zhi,
    out_ref, forcing_ref, xf_ref, xb_ref, yf_ref, yb_ref, zp_ref,
    slots, order, acc, padded, zsc,
):
    count = gather_slots(zlo_p, zmid_p, zhi_p, slots, order)
    spread(slots, order, count, acc)
    for s in range(0, NS, 8):
        for j in range(CJ):
            forcing_ref[pl.ds(s * CJ + j, 8, stride=CJ), :] = acc[s : s + 8, j * CK : (j + 1) * CK]
    stage(
        0.0, 1.0, rows_ref, rows_ref, visc_ref, forcing_ref,
        (xlo, xhi, ylo, yhi, zlo, zhi), padded, zsc, out_ref,
    )
    pack_y(out_ref, yf_ref, yb_ref)
    pack_x(out_ref, xf_ref, xb_ref)
    pack_z(out_ref, zp_ref)


def second_kernel(
    rows_ref, base_ref, visc_ref, forcing_ref, xlo, xhi, ylo, yhi, zlo, zhi,
    out_ref, xf_ref, xb_ref, yf_ref, yb_ref, zp_ref, padded, zsc,
):
    stage(
        0.75, 0.25, rows_ref, base_ref, visc_ref, forcing_ref,
        (xlo, xhi, ylo, yhi, zlo, zhi), padded, zsc, out_ref,
    )
    pack_y(out_ref, yf_ref, yb_ref)
    pack_x(out_ref, xf_ref, xb_ref)
    pack_z(out_ref, zp_ref)


def third_kernel(
    zlo_p, zmid_p, zhi_p, rows_ref, base_ref, visc_ref, forcing_ref, xlo, xhi, ylo, yhi, zlo, zhi,
    out_ref, sampled_ref, slots, order, padded, zsc, field_high, field_low,
):
    stage(
        1.0 / 3.0, 2.0 / 3.0, rows_ref, base_ref, visc_ref, forcing_ref,
        (xlo, xhi, ylo, yhi, zlo, zhi), padded, zsc, out_ref,
    )
    for j in range(CJ):
        for s in range(0, NS, 16):
            value = jnp.concatenate(
                [
                    out_ref[pl.ds(s * CJ + j, 8, stride=CJ), :],
                    out_ref[pl.ds((s + 8) * CJ + j, 8, stride=CJ), :],
                ],
                axis=0,
            )
            high, low = halves(value)
            field_high[s : s + 16, j * CK : (j + 1) * CK] = high
            field_low[s : s + 16, j * CK : (j + 1) * CK] = low
    count = gather_slots(zlo_p, zmid_p, zhi_p, slots, order)
    sampled_ref[...] = jnp.zeros_like(sampled_ref)

    def one_pair(pair, carry):
        block = pair_block(slots, order, pair)
        wx, wy, wz = point_weights(block)
        total = jnp.zeros((NS, 2 * CAP), F32)
        for j in range(0, CJ, 2):
            plane = jnp.concatenate([wz * wy[j : j + 1, :], wz * wy[j + 1 : j + 2, :]], axis=0)
            bh, bl = halves(plane)
            vh = field_high[:, j * CK : (j + 2) * CK]
            vl = field_low[:, j * CK : (j + 2) * CK]
            total = total + lax.dot_general(vh, bh, NN, preferred_element_type=F32)
            total = total + lax.dot_general(vh, bl, NN, preferred_element_type=F32)
            total = total + lax.dot_general(vl, bh, NN, preferred_element_type=F32)
        result = jnp.concatenate(
            [
                jnp.sum(total[c * CI : (c + 1) * CI, :] * wx, axis=0, keepdims=True)
                for c in range(3)
            ]
            + [jnp.zeros((5, 2 * CAP), F32)],
            axis=0,
        )
        sampled_ref[order[2 * pair]] = result[:, :CAP]
        sampled_ref[order[2 * pair + 1]] = result[:, CAP:]
        return carry

    lax.fori_loop(0, (count + 1) // 2, one_pair, 0)


def pick_kernel(tile_ref, low_ref, mid_ref, high_ref, out_ref, slots):
    slots[0:9] = low_ref[...]
    slots[9:18] = mid_ref[...]
    slots[18:27] = high_ref[...]
    for run in range(RUNS):
        code = run_code(tile_ref, run)
        out_ref[:, run * CAP : (run + 1) * CAP] = slots[code, 0:3, :]


def exchanged(forward, backward, axis):
    count = lax.axis_size(axis)
    up = [(i, (i + 1) % count) for i in range(count)]
    down = [(target, source) for source, target in up]
    return lax.ppermute(forward, axis, up), lax.ppermute(backward, axis, down)


def halos_of(xf, xb, yf, yb, zp):
    ylo, yhi = exchanged(yf, yb, "gy")
    xlo, xhi = exchanged(xf, xb, "gx")
    zlo, zhi = exchanged(zp, zp, "gz")
    return xlo, xhi, ylo, yhi, zlo, zhi


FACES = (
    shape(6 * CJ, CK), shape(6 * CJ, CK), shape(2 * NS, CK), shape(2 * NS, CK), shape(6 * CJ, CK),
)
STENCIL_SCRATCH = [
    pltpu.VMEM((3 * (CI + 4) * PAD_ROWS, CK), F32),
    pltpu.VMEM((6 * CJ, CK), F32),
]
SLOT_SCRATCH = [pltpu.VMEM((28, 8, CAP), F32), pltpu.SMEM((32,), jnp.int32)]


def call(kernel, outs, scratch, *args, scalars=0):
    return pl.pallas_call(
        kernel,
        out_shape=outs,
        in_specs=[smem()] * scalars + [vmem()] * (len(args) - scalars),
        out_specs=jax.tree.map(lambda _: vmem(), outs),
        scratch_shapes=scratch,
        compiler_params=params(),
    )(*args)


def per_device(velocity, viscosity, point_force, point_offset, point_cell, point_tile):
    tiles = point_tile.reshape(-1)
    rows = velocity.reshape(NS * CJ, CK)
    visc = viscosity.reshape(CI * CJ, CK)
    cells = point_cell.reshape(RUNS, CAP)

    points, *faces = call(
        pack_kernel, (shape(27, 8, CAP),) + FACES, [],
        tiles, point_force, point_offset, cells, rows, scalars=1,
    )

    halos = halos_of(*faces)
    from_low, from_high = exchanged(points[18:], points[:9], "gx")
    held = jnp.stack([from_low, points[9:18], from_high]).reshape(3, 3, 3, 8, CAP)
    from_low, from_high = exchanged(held[:, 2], held[:, 0], "gy")
    held = jnp.stack([from_low, held[:, 1], from_high])
    mine = held[:, :, 1].reshape(9, 8, CAP)
    from_low, from_high = exchanged(
        held[:, :, 2].reshape(9, 8, CAP), held[:, :, 0].reshape(9, 8, CAP), "gz"
    )
    arrived = (from_low, mine, from_high)

    section_one, forcing, *faces = call(
        first_kernel, (shape(NS * CJ, CK), shape(NS * CJ, CK)) + FACES,
        SLOT_SCRATCH + [pltpu.VMEM((NS, CJ * CK), F32)] + STENCIL_SCRATCH,
        *arrived, rows, visc, *halos,
    )
    section_two, *faces = call(
        second_kernel, (shape(NS * CJ, CK),) + FACES, STENCIL_SCRATCH,
        section_one, rows, visc, forcing, *halos_of(*faces),
    )
    fresh, sampled = call(
        third_kernel, (shape(NS * CJ, CK), shape(28, 8, CAP)),
        SLOT_SCRATCH + STENCIL_SCRATCH + [pltpu.VMEM((NS, CJ * CK), BF16)] * 2,
        *arrived, section_two, rows, visc, forcing, *halos_of(*faces),
    )

    back = sampled[:27].reshape(3, 9, 8, CAP)
    from_low, from_high = exchanged(back[2], back[0], "gz")
    held = jnp.stack([from_low, back[1], from_high]).reshape(3, 3, 3, 8, CAP)
    from_low, from_high = exchanged(held[:, 2], held[:, 0], "gy")
    held = jnp.stack([from_low, held[:, 1], from_high])
    mine = held[:, :, 1].reshape(9, 8, CAP)
    from_low, from_high = exchanged(
        held[:, :, 2].reshape(9, 8, CAP), held[:, :, 0].reshape(9, 8, CAP), "gx"
    )
    point_velocity = call(
        pick_kernel, shape(3, RUNS * CAP), [pltpu.VMEM((27, 8, CAP), F32)],
        tiles, from_low, mine, from_high, scalars=1,
    )
    return fresh.reshape(velocity.shape), point_velocity


def solution(mesh):
    in_specs = (
        P(None, "gx", "gy", "gz"),
        P("gx", "gy", "gz"),
        P(None, ("gx", "gy", "gz")),
        P(None, ("gx", "gy", "gz")),
        P(("gx", "gy", "gz")),
        P(("gx", "gy", "gz"), None),
    )
    out_specs = (P(None, "gx", "gy", "gz"), P(None, ("gx", "gy", "gz")))
    return jax.shard_map(
        per_device, mesh=mesh, in_specs=in_specs, out_specs=out_specs, check_vma=False
    )
```

```python
import functools

import jax
import jax.numpy as jnp
from jax import lax
from jax.experimental import pallas as pl
from jax.experimental.pallas import tpu as pltpu
from jax.sharding import PartitionSpec as P

DT = 0.1
CI, CJ, CK = 64, 16, 128
NS = 3 * CI
CAP = 128
RUNS = 8
NY_DEV, NZ_DEV = 4, 4
UNROLL = 4
PAD_ROWS = 32
F32 = jnp.float32
BF16 = jnp.bfloat16


def vmem():
    return pl.BlockSpec(memory_space=pltpu.VMEM)


def smem():
    return pl.BlockSpec(memory_space=pltpu.SMEM)


def shape(*dims):
    return jax.ShapeDtypeStruct(dims, F32)


def params():
    return pltpu.CompilerParams(vmem_limit_bytes=40 * 1024 * 1024)


def run_code(tile_ref, run):
    target = tile_ref[run * CAP]
    step_a = target // (NY_DEV * NZ_DEV) - lax.axis_index("gx")
    step_b = (target // NZ_DEV) % NY_DEV - lax.axis_index("gy")
    step_c = target % NZ_DEV - lax.axis_index("gz")
    group = 1 - step_a * (1 - 2 * lax.rem(lax.axis_index("gx"), 2))
    return (group * 3 + step_b + 1) * 3 + step_c + 1


def is_even():
    return lax.rem(lax.axis_index("gx"), 2) == 0


def pack_y(rows_ref, forward_ref, backward_ref):
    for r in range(2):
        for s in range(0, NS, 8):
            forward_ref[r * NS + s : r * NS + s + 8, :] = rows_ref[
                pl.ds(s * CJ + CJ - 2 + r, 8, stride=CJ), :
            ]
            backward_ref[r * NS + s : r * NS + s + 8, :] = rows_ref[
                pl.ds(s * CJ + r, 8, stride=CJ), :
            ]


def pack_x(rows_ref, first_ref, second_ref):
    even = is_even()
    for c in range(3):
        base = c * CI * CJ
        upper = rows_ref[base + (CI - 2) * CJ : base + CI * CJ, :]
        lower = rows_ref[base : base + 2 * CJ, :]
        first_ref[c * 2 * CJ : (c + 1) * 2 * CJ, :] = jnp.where(even, upper, lower)
        second_ref[c * 2 * CJ : (c + 1) * 2 * CJ, :] = jnp.where(even, lower, upper)


def z_masks():
    lane = lax.broadcasted_iota(jnp.int32, (CJ, CK), 1)
    return lane


def pack_z(rows_ref, out_ref):
    lane = z_masks()
    group = lane // 4

    def step(t, blocks):
        blocks = list(blocks)
        for r in range(UNROLL):
            u = t * UNROLL + r
            for b in range(6):
                first = pl.multiple_of((b * 32 + u) * CJ, CJ)
                turned = pltpu.roll(rows_ref[pl.ds(first, CJ), :], 2 + 4 * u, 1)
                blocks[b] = jnp.where(group == u, turned, blocks[b])
        return tuple(blocks)

    zero = jnp.zeros((CJ, CK), F32)
    blocks = lax.fori_loop(0, 32 // UNROLL, step, (zero,) * 6)
    for b in range(6):
        out_ref[b * CJ : (b + 1) * CJ, :] = blocks[b]


def pack_kernel(
    tile_ref, force_ref, offset_ref, cell_ref, rows_ref,
    points_ref, xf_ref, xb_ref, yf_ref, yb_ref, zp_ref,
):
    points_ref[...] = jnp.zeros_like(points_ref)
    for run in range(RUNS):
        code = run_code(tile_ref, run)
        lanes = slice(run * CAP, (run + 1) * CAP)
        block = jnp.concatenate(
            [
                force_ref[:, lanes],
                offset_ref[:, lanes],
                cell_ref[run : run + 1, :].astype(F32),
                jnp.ones((1, CAP), F32),
            ],
            axis=0,
        )
        points_ref[code] = block
    pack_y(rows_ref, yf_ref, yb_ref)
    pack_x(rows_ref, xf_ref, xb_ref)
    pack_z(rows_ref, zp_ref)


def weights_along(centre, count):
    middle = lax.broadcasted_iota(jnp.int32, (count, centre.shape[1]), 0).astype(F32) + 0.5
    scaled = (middle - centre) * 0.5
    raw = jnp.exp(-scaled * scaled)
    return raw * (1.0 / jnp.sum(raw, axis=0, keepdims=True))


def point_weights(block):
    cell = block[6:7, :].astype(jnp.int32)
    first = (cell // (CJ * CK)).astype(F32) + block[3:4, :]
    second = ((cell // CK) % CJ).astype(F32) + block[4:5, :]
    third = (cell % CK).astype(F32) + block[5:6, :]
    return weights_along(first, CI), weights_along(second, CJ), weights_along(third, CK)


def halves(value):
    high = value.astype(BF16)
    return high, (value - high.astype(F32)).astype(BF16)


def gather_slots(zlo_ref, zmid_ref, zhi_ref, slots, order):
    filled = jnp.zeros((1, CAP), jnp.int32)
    for group, ref in enumerate((zlo_ref, zmid_ref, zhi_ref)):
        for t in range(9):
            s = group * 9 + t
            value = ref[t]
            slots[s] = value
            filled = filled + jnp.where(value[7:8, :] > 0.5, 1 << s, 0)
    slots[27] = jnp.zeros((8, CAP), F32)
    mask = jnp.max(filled)
    count = jnp.int32(0)
    for s in range(27):
        order[count] = s
        count = count + ((mask >> s) & 1)
    order[count] = 27
    return count


def pair_block(slots, order, pair):
    return jnp.concatenate([slots[order[2 * pair]], slots[order[2 * pair + 1]]], axis=1)


NT = (((1,), (1,)), ((), ()))
NN = (((1,), (0,)), ((), ()))


def spread(slots, order, count, acc):
    acc[...] = jnp.zeros_like(acc)

    def one_pair(pair, carry):
        block = pair_block(slots, order, pair)
        wx, wy, wz = point_weights(block)
        ah, al = halves(jnp.concatenate([block[c : c + 1, :] * wx for c in range(3)], axis=0))
        for j in range(0, CJ, 2):
            plane = jnp.concatenate([wz * wy[j : j + 1, :], wz * wy[j + 1 : j + 2, :]], axis=0)
            bh, bl = halves(plane)
            total = lax.dot_general(ah, bh, NT, preferred_element_type=F32)
            total = total + lax.dot_general(ah, bl, NT, preferred_element_type=F32)
            total = total + lax.dot_general(al, bh, NT, preferred_element_type=F32)
            acc[:, j * CK : (j + 2) * CK] += total
        return carry

    lax.fori_loop(0, (count + 1) // 2, one_pair, 0)


def edge_flags():
    ax, ay, az = (lax.axis_index(n) for n in ("gx", "gy", "gz"))
    nx, ny, nz = (lax.axis_size(n) for n in ("gx", "gy", "gz"))
    return (
        (ax > 0, ax < nx - 1),
        (ay > 0, ay < ny - 1),
        (az > 0, az < nz - 1),
    )


def stage(alpha, beta, rows_ref, base_ref, visc_ref, forcing_ref, halos, padded, zsc, out_ref):
    xa, xb, ylo, yhi, zlo, zhi = halos
    even = is_even()
    (x0, x1), (y0, y1), (z0, z1) = edge_flags()
    step_rows = (CI + 4) * PAD_ROWS
    for c in range(3):
        for r in range(2):
            part = slice((c * 2 + r) * CJ, (c * 2 + r + 1) * CJ)
            lower = jnp.where(even, xb[part, :], xa[part, :])
            upper = jnp.where(even, xa[part, :], xb[part, :])
            for n, (value, ok) in enumerate(((lower, x0), (upper, x1))):
                first = c * step_rows + (n * (CI + 2) + r) * PAD_ROWS + 8
                padded[first : first + CJ, :] = jnp.where(ok, value, 0.0)
        for i in range(0, CI, 8):
            for n, (ref, ok) in enumerate(((ylo, y0), (yhi, y1))):
                for r in range(2):
                    value = ref[r * NS + c * CI + i : r * NS + c * CI + i + 8, :]
                    first = c * step_rows + (i + 2) * PAD_ROWS + (6 + r if n == 0 else 24 + r)
                    padded[pl.ds(first, 8, stride=PAD_ROWS), :] = jnp.where(ok, value, 0.0)
    lane = z_masks()
    low_part = lane % 4 < 2
    for b in range(6):
        part = slice(b * CJ, (b + 1) * CJ)
        zsc[part, :] = jnp.where(
            low_part, jnp.where(z0, zlo[part, :], 0.0), jnp.where(z1, zhi[part, :], 0.0)
        )

    def fill(t, carry):
        for r in range(UNROLL):
            i = t * UNROLL + r
            for c in range(3):
                source = pl.multiple_of((c * CI + i) * CJ, CJ)
                target = pl.multiple_of(c * step_rows + (i + 2) * PAD_ROWS + 8, 8)
                padded[pl.ds(target, CJ), :] = rows_ref[pl.ds(source, CJ), :]
        return carry

    lax.fori_loop(0, CI // UNROLL, fill, 0)

    at0, at01 = lane == 0, lane < 2
    at127, at126 = lane == CK - 1, lane >= CK - 2

    def one_plane(half, u):
        i = half * 32 + u
        visc = (beta * DT) * visc_ref[pl.ds(pl.multiple_of(i * CJ, CJ), CJ), :]
        keep = beta - 6.0 * visc

        def at(c, di, dj):
            first = c * step_rows + (i + 2 + di) * PAD_ROWS + 8 + dj
            return padded[pl.ds(first, CJ), :]

        centre = [at(c, 0, 0) for c in range(3)]
        along = [(beta * DT / 12.0) * value for value in centre]
        for c in range(3):
            here = centre[c]
            block = (2 * c + half) * CJ
            side = pltpu.roll(zsc[block : block + CJ, :], 126 - 4 * u, 1)
            za1 = pltpu.roll(jnp.where(at0, side, here), CK - 1, 1)
            za2 = pltpu.roll(jnp.where(at01, side, here), CK - 2, 1)
            zb1 = pltpu.roll(jnp.where(at127, side, here), 1, 1)
            zb2 = pltpu.roll(jnp.where(at126, side, here), 2, 1)
            xa1, xb1, xa2, xb2 = at(c, 1, 0), at(c, -1, 0), at(c, 2, 0), at(c, -2, 0)
            ya1, yb1, ya2, yb2 = at(c, 0, 1), at(c, 0, -1), at(c, 0, 2), at(c, 0, -2)
            advect = along[0] * (8.0 * (xa1 - xb1) - (xa2 - xb2))
            advect = advect + along[1] * (8.0 * (ya1 - yb1) - (ya2 - yb2))
            advect = advect + along[2] * (8.0 * (za1 - zb1) - (za2 - zb2))
            around = ((xa1 + xb1) + (ya1 + yb1)) + (za1 + zb1)
            where = pl.ds(pl.multiple_of((c * CI + i) * CJ, CJ), CJ)
            fresh = (keep * here + visc * around) - advect + (beta * DT) * forcing_ref[where, :]
            if alpha:
                fresh = fresh + alpha * base_ref[where, :]
            out_ref[where, :] = fresh

    for half in range(2):

        def planes(t, carry, half=half):
            for r in range(UNROLL):
                one_plane(half, t * UNROLL + r)
            return carry

        lax.fori_loop(0, 32 // UNROLL, planes, 0)


def first_kernel(
    zlo_p, zmid_p, zhi_p, rows_ref, visc_ref, xlo, xhi, ylo, yhi, zlo, zhi,
    out_ref, forcing_ref, xf_ref, xb_ref, yf_ref, yb_ref, zp_ref,
    slots, order, acc, padded, zsc,
):
    count = gather_slots(zlo_p, zmid_p, zhi_p, slots, order)
    spread(slots, order, count, acc)
    for s in range(0, NS, 8):
        for j in range(CJ):
            forcing_ref[pl.ds(s * CJ + j, 8, stride=CJ), :] = acc[s : s + 8, j * CK : (j + 1) * CK]
    stage(
        0.0, 1.0, rows_ref, rows_ref, visc_ref, forcing_ref,
        (xlo, xhi, ylo, yhi, zlo, zhi), padded, zsc, out_ref,
    )
    pack_y(out_ref, yf_ref, yb_ref)
    pack_x(out_ref, xf_ref, xb_ref)
    pack_z(out_ref, zp_ref)


def second_kernel(
    rows_ref, base_ref, visc_ref, forcing_ref, xlo, xhi, ylo, yhi, zlo, zhi,
    out_ref, xf_ref, xb_ref, yf_ref, yb_ref, zp_ref, padded, zsc,
):
    stage(
        0.75, 0.25, rows_ref, base_ref, visc_ref, forcing_ref,
        (xlo, xhi, ylo, yhi, zlo, zhi), padded, zsc, out_ref,
    )
    pack_y(out_ref, yf_ref, yb_ref)
    pack_x(out_ref, xf_ref, xb_ref)
    pack_z(out_ref, zp_ref)


def third_kernel(
    zlo_p, zmid_p, zhi_p, rows_ref, base_ref, visc_ref, forcing_ref, xlo, xhi, ylo, yhi, zlo, zhi,
    out_ref, sampled_ref, slots, order, padded, zsc, field_high, field_low,
):
    stage(
        1.0 / 3.0, 2.0 / 3.0, rows_ref, base_ref, visc_ref, forcing_ref,
        (xlo, xhi, ylo, yhi, zlo, zhi), padded, zsc, out_ref,
    )
    for j in range(CJ):
        for s in range(0, NS, 16):
            value = jnp.concatenate(
                [
                    out_ref[pl.ds(s * CJ + j, 8, stride=CJ), :],
                    out_ref[pl.ds((s + 8) * CJ + j, 8, stride=CJ), :],
                ],
                axis=0,
            )
            high, low = halves(value)
            field_high[s : s + 16, j * CK : (j + 1) * CK] = high
            field_low[s : s + 16, j * CK : (j + 1) * CK] = low
    count = gather_slots(zlo_p, zmid_p, zhi_p, slots, order)
    sampled_ref[...] = jnp.zeros_like(sampled_ref)

    def one_pair(pair, carry):
        block = pair_block(slots, order, pair)
        wx, wy, wz = point_weights(block)
        total = jnp.zeros((NS, 2 * CAP), F32)
        for j in range(0, CJ, 2):
            plane = jnp.concatenate([wz * wy[j : j + 1, :], wz * wy[j + 1 : j + 2, :]], axis=0)
            bh, bl = halves(plane)
            vh = field_high[:, j * CK : (j + 2) * CK]
            vl = field_low[:, j * CK : (j + 2) * CK]
            total = total + lax.dot_general(vh, bh, NN, preferred_element_type=F32)
            total = total + lax.dot_general(vh, bl, NN, preferred_element_type=F32)
            total = total + lax.dot_general(vl, bh, NN, preferred_element_type=F32)
        result = jnp.concatenate(
            [
                jnp.sum(total[c * CI : (c + 1) * CI, :] * wx, axis=0, keepdims=True)
                for c in range(3)
            ]
            + [jnp.zeros((5, 2 * CAP), F32)],
            axis=0,
        )
        sampled_ref[order[2 * pair]] = result[:, :CAP]
        sampled_ref[order[2 * pair + 1]] = result[:, CAP:]
        return carry

    lax.fori_loop(0, (count + 1) // 2, one_pair, 0)


def pick_kernel(tile_ref, low_ref, mid_ref, high_ref, out_ref, slots):
    slots[0:9] = low_ref[...]
    slots[9:18] = mid_ref[...]
    slots[18:27] = high_ref[...]
    for run in range(RUNS):
        code = run_code(tile_ref, run)
        out_ref[:, run * CAP : (run + 1) * CAP] = slots[code, 0:3, :]


def exchanged(forward, backward, axis):
    count = lax.axis_size(axis)
    up = [(i, (i + 1) % count) for i in range(count)]
    down = [(target, source) for source, target in up]
    return lax.ppermute(forward, axis, up), lax.ppermute(backward, axis, down)


def swapped(first, second, axis):
    count = lax.axis_size(axis)
    pairs = [[], []]
    for start in range(2):
        for i in range(start, count, 2):
            pairs[start] += [(i, (i + 1) % count), ((i + 1) % count, i)]
    return lax.ppermute(first, axis, pairs[0]), lax.ppermute(second, axis, pairs[1])


def halos_of(xf, xb, yf, yb, zp):
    ylo, yhi = exchanged(yf, yb, "gy")
    xlo, xhi = swapped(xf, xb, "gx")
    zlo, zhi = exchanged(zp, zp, "gz")
    return xlo, xhi, ylo, yhi, zlo, zhi


FACES = (
    shape(6 * CJ, CK), shape(6 * CJ, CK), shape(2 * NS, CK), shape(2 * NS, CK), shape(6 * CJ, CK),
)
STENCIL_SCRATCH = [
    pltpu.VMEM((3 * (CI + 4) * PAD_ROWS, CK), F32),
    pltpu.VMEM((6 * CJ, CK), F32),
]
SLOT_SCRATCH = [pltpu.VMEM((28, 8, CAP), F32), pltpu.SMEM((32,), jnp.int32)]


def call(kernel, outs, scratch, *args, scalars=0):
    return pl.pallas_call(
        kernel,
        out_shape=outs,
        in_specs=[smem()] * scalars + [vmem()] * (len(args) - scalars),
        out_specs=jax.tree.map(lambda _: vmem(), outs),
        scratch_shapes=scratch,
        compiler_params=params(),
    )(*args)


def per_device(velocity, viscosity, point_force, point_offset, point_cell, point_tile):
    tiles = point_tile.reshape(-1)
    rows = velocity.reshape(NS * CJ, CK)
    visc = viscosity.reshape(CI * CJ, CK)
    cells = point_cell.reshape(RUNS, CAP)

    points, *faces = call(
        pack_kernel, (shape(27, 8, CAP),) + FACES, [],
        tiles, point_force, point_offset, cells, rows, scalars=1,
    )

    halos = halos_of(*faces)
    from_first, from_second = swapped(points[:9], points[18:], "gx")
    held = jnp.stack([from_first, points[9:18], from_second]).reshape(3, 3, 3, 8, CAP)
    from_low, from_high = exchanged(held[:, 2], held[:, 0], "gy")
    held = jnp.stack([from_low, held[:, 1], from_high])
    mine = held[:, :, 1].reshape(9, 8, CAP)
    from_low, from_high = exchanged(
        held[:, :, 2].reshape(9, 8, CAP), held[:, :, 0].reshape(9, 8, CAP), "gz"
    )
    arrived = (from_low, mine, from_high)

    section_one, forcing, *faces = call(
        first_kernel, (shape(NS * CJ, CK), shape(NS * CJ, CK)) + FACES,
        SLOT_SCRATCH + [pltpu.VMEM((NS, CJ * CK), F32)] + STENCIL_SCRATCH,
        *arrived, rows, visc, *halos,
    )
    section_two, *faces = call(
        second_kernel, (shape(NS * CJ, CK),) + FACES, STENCIL_SCRATCH,
        section_one, rows, visc, forcing, *halos_of(*faces),
    )
    fresh, sampled = call(
        third_kernel, (shape(NS * CJ, CK), shape(28, 8, CAP)),
        SLOT_SCRATCH + STENCIL_SCRATCH + [pltpu.VMEM((NS, CJ * CK), BF16)] * 2,
        *arrived, section_two, rows, visc, forcing, *halos_of(*faces),
    )

    back = sampled[:27].reshape(3, 9, 8, CAP)
    from_low, from_high = exchanged(back[2], back[0], "gz")
    held = jnp.stack([from_low, back[1], from_high]).reshape(3, 3, 3, 8, CAP)
    from_low, from_high = exchanged(held[:, 2], held[:, 0], "gy")
    held = jnp.stack([from_low, held[:, 1], from_high])
    mine = held[:, :, 1].reshape(9, 8, CAP)
    from_first, from_second = swapped(
        held[:, :, 0].reshape(9, 8, CAP), held[:, :, 2].reshape(9, 8, CAP), "gx"
    )
    point_velocity = call(
        pick_kernel, shape(3, RUNS * CAP), [pltpu.VMEM((27, 8, CAP), F32)],
        tiles, from_first, mine, from_second, scalars=1,
    )
    return fresh.reshape(velocity.shape), point_velocity


def solution(mesh):
    in_specs = (
        P(None, "gx", "gy", "gz"),
        P("gx", "gy", "gz"),
        P(None, ("gx", "gy", "gz")),
        P(None, ("gx", "gy", "gz")),
        P(("gx", "gy", "gz")),
        P(("gx", "gy", "gz"), None),
    )
    out_specs = (P(None, "gx", "gy", "gz"), P(None, ("gx", "gy", "gz")))
    return jax.shard_map(
        per_device, mesh=mesh, in_specs=in_specs, out_specs=out_specs, check_vma=False
    )
```

```python
import functools

import jax
import jax.numpy as jnp
from jax import lax
from jax.experimental import pallas as pl
from jax.experimental.pallas import tpu as pltpu
from jax.sharding import PartitionSpec as P

DT = 0.1
CI, CJ, CK = 64, 16, 128
NS = 3 * CI
CAP = 128
RUNS = 8
NY_DEV, NZ_DEV = 4, 4
UNROLL = 4
SLOT_ROWS = 9 * 8
SPREAD_PARTS = 2
SAMPLE_PARTS = 2
PAD_ROWS = 32
F32 = jnp.float32
BF16 = jnp.bfloat16


def vmem():
    return pl.BlockSpec(memory_space=pltpu.VMEM)


def shape(*dims):
    return jax.ShapeDtypeStruct(dims, F32)


def params():
    return pltpu.CompilerParams(vmem_limit_bytes=40 * 1024 * 1024)


def run_code(tile_ref, run):
    target = tile_ref[run * CAP]
    step_a = target // (NY_DEV * NZ_DEV) - lax.axis_index("gx")
    step_b = (target // NZ_DEV) % NY_DEV - lax.axis_index("gy")
    step_c = target % NZ_DEV - lax.axis_index("gz")
    group = 1 - step_a * (1 - 2 * lax.rem(lax.axis_index("gx"), 2))
    return (group * 3 + step_b + 1) * 3 + step_c + 1


def is_even():
    return lax.rem(lax.axis_index("gx"), 2) == 0


def pack_y(rows_ref, forward_ref, backward_ref):
    for r in range(2):
        for s in range(0, NS, 8):
            forward_ref[r * NS + s : r * NS + s + 8, :] = rows_ref[
                pl.ds(s * CJ + CJ - 2 + r, 8, stride=CJ), :
            ]
            backward_ref[r * NS + s : r * NS + s + 8, :] = rows_ref[
                pl.ds(s * CJ + r, 8, stride=CJ), :
            ]


def pack_x(rows_ref, first_ref, second_ref, skip=0):
    even = is_even()
    for c in range(3):
        base = c * CI * CJ
        upper = rows_ref[base + (CI - 2) * CJ : base + CI * CJ, :]
        lower = rows_ref[base : base + 2 * CJ, :]
        part = slice(skip + c * 2 * CJ, skip + (c + 1) * 2 * CJ)
        first_ref[part, :] = jnp.where(even, upper, lower)
        second_ref[part, :] = jnp.where(even, lower, upper)


def z_masks():
    lane = lax.broadcasted_iota(jnp.int32, (CJ, CK), 1)
    return lane


def pack_z(rows_ref, out_ref):
    lane = z_masks()
    group = lane // 4

    def step(t, blocks):
        blocks = list(blocks)
        for r in range(UNROLL):
            u = t * UNROLL + r
            for b in range(6):
                first = pl.multiple_of((b * 32 + u) * CJ, CJ)
                turned = pltpu.roll(rows_ref[pl.ds(first, CJ), :], 2 + 4 * u, 1)
                blocks[b] = jnp.where(group == u, turned, blocks[b])
        return tuple(blocks)

    zero = jnp.zeros((CJ, CK), F32)
    blocks = lax.fori_loop(0, 32 // UNROLL, step, (zero,) * 6)
    for b in range(6):
        out_ref[b * CJ : (b + 1) * CJ, :] = blocks[b]


def pack_kernel(
    tile_any, force_any, offset_any, cell_any, rows_any,
    mid_ref, code_ref, xa_ref, xb_ref, yf_ref, yb_ref, zp_ref,
    points_ref, tile_ref, force_ref, offset_ref, cell_ref, rows_ref, sems,
):
    moves = [
        pltpu.make_async_copy(source, target, sems.at[n])
        for n, (source, target) in enumerate(
            (
                (tile_any, tile_ref), (force_any, force_ref), (offset_any, offset_ref),
                (cell_any, cell_ref), (rows_any, rows_ref),
            )
        )
    ]
    for move in moves:
        move.start()
    points_ref[...] = jnp.zeros_like(points_ref)
    for move in moves[:4]:
        move.wait()
    for run in range(RUNS):
        code = run_code(tile_ref, run)
        lanes = slice(run * CAP, (run + 1) * CAP)
        block = jnp.concatenate(
            [
                force_ref[:, lanes],
                offset_ref[:, lanes],
                cell_ref[run : run + 1, :].astype(F32),
                jnp.ones((1, CAP), F32),
            ],
            axis=0,
        )
        points_ref[code] = block
        code_ref[run : run + 1, :] = jnp.full((1, CAP), code, jnp.int32)
    for group, ref in enumerate((xa_ref, mid_ref, xb_ref)):
        for t in range(9):
            ref[t * 8 : (t + 1) * 8, :] = points_ref[group * 9 + t]
    moves[4].wait()
    pack_y(rows_ref, yf_ref, yb_ref)
    pack_x(rows_ref, xa_ref, xb_ref, SLOT_ROWS)
    pack_z(rows_ref, zp_ref)


def weights_along(centre, count):
    middle = lax.broadcasted_iota(jnp.int32, (count, centre.shape[1]), 0).astype(F32) + 0.5
    scaled = (middle - centre) * 0.5
    raw = jnp.exp(-scaled * scaled)
    return raw * (1.0 / jnp.sum(raw, axis=0, keepdims=True))


def point_weights(block):
    cell = block[6:7, :].astype(jnp.int32)
    first = (cell // (CJ * CK)).astype(F32) + block[3:4, :]
    second = ((cell // CK) % CJ).astype(F32) + block[4:5, :]
    third = (cell % CK).astype(F32) + block[5:6, :]
    return weights_along(first, CI), weights_along(second, CJ), weights_along(third, CK)


def halves(value):
    high = value.astype(BF16)
    return high, (value - high.astype(F32)).astype(BF16)


def gather_slots(zlo_ref, zmid_ref, zhi_ref, slots, order):
    filled = jnp.zeros((1, CAP), jnp.int32)
    for group, ref in enumerate((zlo_ref, zmid_ref, zhi_ref)):
        for t in range(9):
            s = group * 9 + t
            value = ref[t * 8 : (t + 1) * 8, :]
            slots[s] = value
            filled = filled + jnp.where(value[7:8, :] > 0.5, 1 << s, 0)
    slots[27] = jnp.zeros((8, CAP), F32)
    mask = jnp.max(filled)
    count = jnp.int32(0)
    for s in range(27):
        order[count] = s
        count = count + ((mask >> s) & 1)
    order[count] = 27
    return count


def pair_block(slots, order, pair):
    return jnp.concatenate([slots[order[2 * pair]], slots[order[2 * pair + 1]]], axis=1)


NT = (((1,), (1,)), ((), ()))
NN = (((1,), (0,)), ((), ()))


def spread(slots, order, count, plane, forcing_ref):
    forcing_ref[...] = jnp.zeros_like(forcing_ref)
    width = 2 * CAP

    def one_pair(pair, carry):
        block = pair_block(slots, order, pair)
        wx, wy, wz = point_weights(block)
        for i in range(CI):
            high, low = halves(wx[i : i + 1, :] * wy)
            plane[i * CJ : (i + 1) * CJ, :width] = high
            plane[i * CJ : (i + 1) * CJ, width:] = low
        parts = [halves(block[c : c + 1, :] * wz) for c in range(3)]
        both_high = jnp.concatenate([parts[0][0], parts[1][0]], axis=0)
        both_low = jnp.concatenate([parts[0][1], parts[1][1]], axis=0)
        third = jnp.concatenate(parts[2], axis=0)

        def dot(a, b):
            return lax.dot_general(a, b, NT, preferred_element_type=F32)

        step = CI * CJ // SPREAD_PARTS
        for m in range(0, CI * CJ, step):
            high, low = plane[m : m + step, :width], plane[m : m + step, width:]
            pairs = dot(high, both_high) + dot(low, both_high) + dot(high, both_low)
            last = dot(high, third) + dot(low, third)
            for c in range(2):
                first = c * CI * CJ + m
                forcing_ref[first : first + step, :] += pairs[:, c * CK : (c + 1) * CK]
            first = 2 * CI * CJ + m
            forcing_ref[first : first + step, :] += last[:, :CK] + last[:, CK:]
        return carry

    lax.fori_loop(0, (count + 1) // 2, one_pair, 0)


def sample(slots, order, count, field, sampled_ref):
    def one_pair(pair, carry):
        block = pair_block(slots, order, pair)
        wx, wy, wz = point_weights(block)
        high, low = halves(wz)
        high = jnp.concatenate([high, high], axis=0)
        step = CI * CJ // SAMPLE_PARTS
        sums = [jnp.zeros((CJ, 2 * CAP), F32)] * 3
        for m in range(0, CI * CJ, step):
            for c in range(3):
                part = slice(c * CI * CJ + m, c * CI * CJ + m + step)
                along = lax.dot_general(field[part, :], high, NN, preferred_element_type=F32)
                along = along + lax.dot_general(
                    field[part, :CK], low, NN, preferred_element_type=F32
                )
                for t in range(step // CJ):
                    i = m // CJ + t
                    sums[c] = sums[c] + along[t * CJ : (t + 1) * CJ, :] * wx[i : i + 1, :]
        rows = [jnp.sum(sums[c] * wy, axis=0, keepdims=True) for c in range(3)]
        result = jnp.concatenate(rows + [jnp.zeros((5, 2 * CAP), F32)], axis=0)
        sampled_ref[order[2 * pair]] = result[:, :CAP]
        sampled_ref[order[2 * pair + 1]] = result[:, CAP:]
        return carry

    lax.fori_loop(0, (count + 1) // 2, one_pair, 0)


def edge_flags():
    ax, ay, az = (lax.axis_index(n) for n in ("gx", "gy", "gz"))
    nx, ny, nz = (lax.axis_size(n) for n in ("gx", "gy", "gz"))
    return (
        (ax > 0, ax < nx - 1),
        (ay > 0, ay < ny - 1),
        (az > 0, az < nz - 1),
    )


def stage(
    alpha, beta, rows_ref, base_ref, visc_ref, forcing_ref, halos, padded, zsc, out_ref, skip=0
):
    xa, xb, ylo, yhi, zlo, zhi = halos
    even = is_even()
    (x0, x1), (y0, y1), (z0, z1) = edge_flags()
    step_rows = (CI + 4) * PAD_ROWS
    for c in range(3):
        for r in range(2):
            part = slice(skip + (c * 2 + r) * CJ, skip + (c * 2 + r + 1) * CJ)
            lower = jnp.where(even, xb[part, :], xa[part, :])
            upper = jnp.where(even, xa[part, :], xb[part, :])
            for n, (value, ok) in enumerate(((lower, x0), (upper, x1))):
                first = c * step_rows + (n * (CI + 2) + r) * PAD_ROWS + 8
                padded[first : first + CJ, :] = jnp.where(ok, value, 0.0)
        for i in range(0, CI, 8):
            for n, (ref, ok) in enumerate(((ylo, y0), (yhi, y1))):
                for r in range(2):
                    value = ref[r * NS + c * CI + i : r * NS + c * CI + i + 8, :]
                    first = c * step_rows + (i + 2) * PAD_ROWS + (6 + r if n == 0 else 24 + r)
                    padded[pl.ds(first, 8, stride=PAD_ROWS), :] = jnp.where(ok, value, 0.0)
    lane = z_masks()
    low_part = lane % 4 < 2
    for b in range(6):
        part = slice(skip + b * CJ, skip + (b + 1) * CJ)
        zsc[b * CJ : (b + 1) * CJ, :] = jnp.where(
            low_part, jnp.where(z0, zlo[part, :], 0.0), jnp.where(z1, zhi[part, :], 0.0)
        )

    def fill(t, carry):
        for r in range(UNROLL):
            i = t * UNROLL + r
            for c in range(3):
                source = pl.multiple_of((c * CI + i) * CJ, CJ)
                target = pl.multiple_of(c * step_rows + (i + 2) * PAD_ROWS + 8, 8)
                padded[pl.ds(target, CJ), :] = rows_ref[pl.ds(source, CJ), :]
        return carry

    lax.fori_loop(0, CI // UNROLL, fill, 0)

    at0, at01 = lane == 0, lane < 2
    at127, at126 = lane == CK - 1, lane >= CK - 2

    def one_plane(half, u):
        i = half * 32 + u
        visc = (beta * DT) * visc_ref[pl.ds(pl.multiple_of(i * CJ, CJ), CJ), :]
        keep = beta - 6.0 * visc

        def at(c, di, dj):
            first = c * step_rows + (i + 2 + di) * PAD_ROWS + 8 + dj
            return padded[pl.ds(first, CJ), :]

        centre = [at(c, 0, 0) for c in range(3)]
        along = [(beta * DT / 12.0) * value for value in centre]
        for c in range(3):
            here = centre[c]
            block = (2 * c + half) * CJ
            side = pltpu.roll(zsc[block : block + CJ, :], 126 - 4 * u, 1)
            za1 = pltpu.roll(jnp.where(at0, side, here), CK - 1, 1)
            za2 = pltpu.roll(jnp.where(at01, side, here), CK - 2, 1)
            zb1 = pltpu.roll(jnp.where(at127, side, here), 1, 1)
            zb2 = pltpu.roll(jnp.where(at126, side, here), 2, 1)
            xa1, xb1, xa2, xb2 = at(c, 1, 0), at(c, -1, 0), at(c, 2, 0), at(c, -2, 0)
            ya1, yb1, ya2, yb2 = at(c, 0, 1), at(c, 0, -1), at(c, 0, 2), at(c, 0, -2)
            advect = along[0] * (8.0 * (xa1 - xb1) - (xa2 - xb2))
            advect = advect + along[1] * (8.0 * (ya1 - yb1) - (ya2 - yb2))
            advect = advect + along[2] * (8.0 * (za1 - zb1) - (za2 - zb2))
            around = ((xa1 + xb1) + (ya1 + yb1)) + (za1 + zb1)
            where = pl.ds(pl.multiple_of((c * CI + i) * CJ, CJ), CJ)
            fresh = (keep * here + visc * around) - advect + (beta * DT) * forcing_ref[where, :]
            if alpha:
                fresh = fresh + alpha * base_ref[where, :]
            out_ref[where, :] = fresh

    for half in range(2):

        def planes(t, carry, half=half):
            for r in range(UNROLL):
                one_plane(half, t * UNROLL + r)
            return carry

        lax.fori_loop(0, 32 // UNROLL, planes, 0)


def first_kernel(
    zlo, zmid, zhi, rows_ref, visc_ref, xlo, xhi, ylo, yhi,
    out_ref, forcing_ref, xf_ref, xb_ref, yf_ref, yb_ref, zp_ref,
    slots, order, plane, padded, zsc,
):
    count = gather_slots(zlo, zmid, zhi, slots, order)
    spread(slots, order, count, plane, forcing_ref)
    stage(
        0.0, 1.0, rows_ref, rows_ref, visc_ref, forcing_ref,
        (xlo, xhi, ylo, yhi, zlo, zhi), padded, zsc, out_ref, SLOT_ROWS,
    )
    pack_y(out_ref, yf_ref, yb_ref)
    pack_x(out_ref, xf_ref, xb_ref)
    pack_z(out_ref, zp_ref)


def second_kernel(
    rows_ref, base_ref, visc_ref, forcing_ref, xlo, xhi, ylo, yhi, zlo, zhi,
    out_ref, xf_ref, xb_ref, yf_ref, yb_ref, zp_ref, padded, zsc,
):
    stage(
        0.75, 0.25, rows_ref, base_ref, visc_ref, forcing_ref,
        (xlo, xhi, ylo, yhi, zlo, zhi), padded, zsc, out_ref,
    )
    pack_y(out_ref, yf_ref, yb_ref)
    pack_x(out_ref, xf_ref, xb_ref)
    pack_z(out_ref, zp_ref)


def third_kernel(
    zlo_p, zmid_p, zhi_p, rows_ref, base_ref, visc_ref, forcing_ref, xlo, xhi, ylo, yhi, zlo, zhi,
    out_ref, sampled_ref, slots, order, padded, zsc, field,
):
    stage(
        1.0 / 3.0, 2.0 / 3.0, rows_ref, base_ref, visc_ref, forcing_ref,
        (xlo, xhi, ylo, yhi, zlo, zhi), padded, zsc, out_ref,
    )
    def split(t, carry):
        first = pl.multiple_of(t * 256, 256)
        high, low = halves(out_ref[pl.ds(first, 256), :])
        field[pl.ds(first, 256), :CK] = high
        field[pl.ds(first, 256), CK:] = low
        return carry

    lax.fori_loop(0, NS * CJ // 256, split, 0)
    count = gather_slots(zlo_p, zmid_p, zhi_p, slots, order)
    sampled_ref[...] = jnp.zeros_like(sampled_ref)
    sample(slots, order, count, field, sampled_ref)


def pick_kernel(code_ref, low_ref, mid_ref, high_ref, out_ref):
    picked = [jnp.zeros((3, CAP), F32)] * RUNS
    for group, ref in enumerate((low_ref, mid_ref, high_ref)):
        for t in range(9):
            value = ref[t][:3, :]
            for run in range(RUNS):
                mine = code_ref[run : run + 1, :] == group * 9 + t
                picked[run] = jnp.where(mine, value, picked[run])
    for run in range(RUNS):
        out_ref[:, run * CAP : (run + 1) * CAP] = picked[run]


def exchanged(forward, backward, axis):
    count = lax.axis_size(axis)
    up = [(i, (i + 1) % count) for i in range(count)]
    down = [(target, source) for source, target in up]
    return lax.ppermute(forward, axis, up), lax.ppermute(backward, axis, down)


def swapped(first, second, axis):
    count = lax.axis_size(axis)
    pairs = [[], []]
    for start in range(2):
        for i in range(start, count, 2):
            pairs[start] += [(i, (i + 1) % count), ((i + 1) % count, i)]
    return lax.ppermute(first, axis, pairs[0]), lax.ppermute(second, axis, pairs[1])


def halos_of(xf, xb, yf, yb, zp):
    ylo, yhi = exchanged(yf, yb, "gy")
    xlo, xhi = swapped(xf, xb, "gx")
    zlo, zhi = exchanged(zp, zp, "gz")
    return xlo, xhi, ylo, yhi, zlo, zhi


FACES = (
    shape(6 * CJ, CK), shape(6 * CJ, CK), shape(2 * NS, CK), shape(2 * NS, CK), shape(6 * CJ, CK),
)
STENCIL_SCRATCH = [
    pltpu.VMEM((3 * (CI + 4) * PAD_ROWS, CK), F32),
    pltpu.VMEM((6 * CJ, CK), F32),
]
SLOT_SCRATCH = [pltpu.VMEM((28, 8, CAP), F32), pltpu.SMEM((32,), jnp.int32)]


def call(kernel, outs, scratch, *args, in_place=False):
    if in_place:
        args = [pltpu.with_memory_space_constraint(a, pltpu.HBM) for a in args]
    return pl.pallas_call(
        kernel,
        out_shape=outs,
        in_specs=[pl.BlockSpec(memory_space=pltpu.HBM) if in_place else vmem()] * len(args),
        out_specs=jax.tree.map(lambda _: vmem(), outs),
        scratch_shapes=scratch,
        compiler_params=params(),
    )(*args)


def per_device(velocity, viscosity, point_force, point_offset, point_cell, point_tile):
    tiles = point_tile.reshape(-1)
    rows = velocity.reshape(NS * CJ, CK)
    visc = viscosity.reshape(CI * CJ, CK)
    cells = point_cell.reshape(RUNS, CAP)

    message = shape(SLOT_ROWS + 6 * CJ, CK)
    mid, codes, xa, xb, yf, yb, zp = call(
        pack_kernel,
        (shape(SLOT_ROWS, CAP), jax.ShapeDtypeStruct((RUNS, CAP), jnp.int32), message, message)
        + FACES[2:],
        [
            pltpu.VMEM((27, 8, CAP), F32),
            pltpu.SMEM((RUNS * CAP,), jnp.int32),
            pltpu.VMEM((3, RUNS * CAP), F32),
            pltpu.VMEM((3, RUNS * CAP), F32),
            pltpu.VMEM((RUNS, CAP), jnp.int32),
            pltpu.VMEM((NS * CJ, CK), F32),
            pltpu.SemaphoreType.DMA((5,)),
        ],
        tiles, point_force, point_offset, cells, rows, in_place=True,
    )

    def slots_of(received):
        return received[:SLOT_ROWS]

    xa, xb = swapped(xa, xb, "gx")
    ylo, yhi = exchanged(yf, yb, "gy")
    held = jnp.stack([slots_of(xa), mid, slots_of(xb)]).reshape(3, 3, 3, 8, CAP)
    from_low, from_high = exchanged(held[:, 2], held[:, 0], "gy")
    held = jnp.stack([from_low, held[:, 1], from_high])
    mine = held[:, :, 1].reshape(SLOT_ROWS, CAP)
    zlo, zhi = exchanged(
        jnp.concatenate([held[:, :, 2].reshape(SLOT_ROWS, CAP), zp]),
        jnp.concatenate([held[:, :, 0].reshape(SLOT_ROWS, CAP), zp]),
        "gz",
    )
    arrived = (zlo, mine, zhi)

    section_one, forcing, *faces = call(
        first_kernel, (shape(NS * CJ, CK), shape(NS * CJ, CK)) + FACES,
        SLOT_SCRATCH + [pltpu.VMEM((CI * CJ, 4 * CAP), BF16)] + STENCIL_SCRATCH,
        *arrived, rows, visc, xa, xb, ylo, yhi,
    )
    section_two, *faces = call(
        second_kernel, (shape(NS * CJ, CK),) + FACES, STENCIL_SCRATCH,
        section_one, rows, visc, forcing, *halos_of(*faces),
    )
    fresh, sampled = call(
        third_kernel, (shape(NS * CJ, CK), shape(28, 8, CAP)),
        SLOT_SCRATCH + STENCIL_SCRATCH + [pltpu.VMEM((NS * CJ, 2 * CK), BF16)],
        *arrived, section_two, rows, visc, forcing, *halos_of(*faces),
    )

    back = sampled[:27].reshape(3, 9, 8, CAP)
    from_low, from_high = exchanged(back[2], back[0], "gz")
    held = jnp.stack([from_low, back[1], from_high]).reshape(3, 3, 3, 8, CAP)
    from_low, from_high = exchanged(held[:, 2], held[:, 0], "gy")
    held = jnp.stack([from_low, held[:, 1], from_high])
    mine = held[:, :, 1].reshape(9, 8, CAP)
    from_first, from_second = swapped(
        held[:, :, 0].reshape(9, 8, CAP), held[:, :, 2].reshape(9, 8, CAP), "gx"
    )
    point_velocity = call(
        pick_kernel, shape(3, RUNS * CAP), [],
        codes, from_first, mine, from_second,
    )
    return fresh.reshape(velocity.shape), point_velocity


def solution(mesh):
    in_specs = (
        P(None, "gx", "gy", "gz"),
        P("gx", "gy", "gz"),
        P(None, ("gx", "gy", "gz")),
        P(None, ("gx", "gy", "gz")),
        P(("gx", "gy", "gz")),
        P(("gx", "gy", "gz"), None),
    )
    out_specs = (P(None, "gx", "gy", "gz"), P(None, ("gx", "gy", "gz")))
    return jax.shard_map(
        per_device, mesh=mesh, in_specs=in_specs, out_specs=out_specs, check_vma=False
    )
```

```python
import functools

import jax
import jax.numpy as jnp
from jax import lax
from jax.experimental import pallas as pl
from jax.experimental.pallas import tpu as pltpu
from jax.sharding import PartitionSpec as P

DT = 0.1
CI, CJ, CK = 64, 16, 128
NS = 3 * CI
CAP = 128
RUNS = 8
NY_DEV, NZ_DEV = 4, 4
UNROLL = 4
PACK_UNROLL = 8
SLOT_ROWS = 9 * 8
SPREAD_PARTS = 2
SAMPLE_PARTS = 2
PAD_ROWS = 32
F32 = jnp.float32
BF16 = jnp.bfloat16


def vmem():
    return pl.BlockSpec(memory_space=pltpu.VMEM)


def shape(*dims):
    return jax.ShapeDtypeStruct(dims, F32)


def params():
    return pltpu.CompilerParams(vmem_limit_bytes=40 * 1024 * 1024)


def run_code(tile_ref, run):
    target = tile_ref[run * CAP]
    step_a = target // (NY_DEV * NZ_DEV) - lax.axis_index("gx")
    step_b = (target // NZ_DEV) % NY_DEV - lax.axis_index("gy")
    step_c = target % NZ_DEV - lax.axis_index("gz")
    group = 1 - step_a * (1 - 2 * lax.rem(lax.axis_index("gx"), 2))
    return (group * 3 + step_b + 1) * 3 + step_c + 1


def is_even():
    return lax.rem(lax.axis_index("gx"), 2) == 0


def pack_y(rows_ref, forward_ref, backward_ref):
    for r in range(2):
        for s in range(0, NS, 8):
            forward_ref[r * NS + s : r * NS + s + 8, :] = rows_ref[
                pl.ds(s * CJ + CJ - 2 + r, 8, stride=CJ), :
            ]
            backward_ref[r * NS + s : r * NS + s + 8, :] = rows_ref[
                pl.ds(s * CJ + r, 8, stride=CJ), :
            ]


def pack_x(rows_ref, first_ref, second_ref, skip=0):
    even = is_even()
    for c in range(3):
        base = c * CI * CJ
        upper = rows_ref[base + (CI - 2) * CJ : base + CI * CJ, :]
        lower = rows_ref[base : base + 2 * CJ, :]
        part = slice(skip + c * 2 * CJ, skip + (c + 1) * 2 * CJ)
        first_ref[part, :] = jnp.where(even, upper, lower)
        second_ref[part, :] = jnp.where(even, lower, upper)


def z_masks():
    lane = lax.broadcasted_iota(jnp.int32, (CJ, CK), 1)
    return lane


def pack_z(rows_ref, out_ref):
    lane = z_masks()
    group = lane // 4

    def step(t, blocks):
        blocks = list(blocks)
        for r in range(PACK_UNROLL):
            u = t * PACK_UNROLL + r
            for b in range(6):
                first = pl.multiple_of((b * 32 + u) * CJ, CJ)
                turned = pltpu.roll(rows_ref[pl.ds(first, CJ), :], 2 + 4 * u, 1)
                blocks[b] = jnp.where(group == u, turned, blocks[b])
        return tuple(blocks)

    zero = jnp.zeros((CJ, CK), F32)
    blocks = lax.fori_loop(0, 32 // PACK_UNROLL, step, (zero,) * 6)
    for b in range(6):
        out_ref[b * CJ : (b + 1) * CJ, :] = blocks[b]


def pack_kernel(
    tile_any, force_any, offset_any, cell_any, rows_any,
    mid_ref, code_ref, xa_ref, xb_ref, yf_ref, yb_ref, zp_ref,
    points_ref, tile_ref, force_ref, offset_ref, cell_ref, rows_ref, sems,
):
    moves = [
        pltpu.make_async_copy(source, target, sems.at[n])
        for n, (source, target) in enumerate(
            (
                (tile_any, tile_ref), (force_any, force_ref), (offset_any, offset_ref),
                (cell_any, cell_ref), (rows_any, rows_ref),
            )
        )
    ]
    for move in moves:
        move.start()
    points_ref[...] = jnp.zeros_like(points_ref)
    for move in moves[:4]:
        move.wait()
    for run in range(RUNS):
        code = run_code(tile_ref, run)
        lanes = slice(run * CAP, (run + 1) * CAP)
        block = jnp.concatenate(
            [
                force_ref[:, lanes],
                offset_ref[:, lanes],
                cell_ref[run : run + 1, :].astype(F32),
                jnp.ones((1, CAP), F32),
            ],
            axis=0,
        )
        points_ref[code] = block
        code_ref[run : run + 1, :] = jnp.full((1, CAP), code, jnp.int32)
    for group, ref in enumerate((xa_ref, mid_ref, xb_ref)):
        for t in range(9):
            ref[t * 8 : (t + 1) * 8, :] = points_ref[group * 9 + t]
    moves[4].wait()
    pack_y(rows_ref, yf_ref, yb_ref)
    pack_x(rows_ref, xa_ref, xb_ref, SLOT_ROWS)
    pack_z(rows_ref, zp_ref)


def weights_along(centre, count):
    middle = lax.broadcasted_iota(jnp.int32, (count, centre.shape[1]), 0).astype(F32) + 0.5
    scaled = (middle - centre) * 0.5
    raw = jnp.exp(-scaled * scaled)
    return raw * (1.0 / jnp.sum(raw, axis=0, keepdims=True))


def point_weights(block):
    cell = block[6:7, :].astype(jnp.int32)
    first = (cell // (CJ * CK)).astype(F32) + block[3:4, :]
    second = ((cell // CK) % CJ).astype(F32) + block[4:5, :]
    third = (cell % CK).astype(F32) + block[5:6, :]
    return weights_along(first, CI), weights_along(second, CJ), weights_along(third, CK)


def halves(value):
    high = value.astype(BF16)
    return high, (value - high.astype(F32)).astype(BF16)


def gather_slots(refs, slots, order):
    filled = jnp.zeros((1, CAP), jnp.int32)
    for group, ref in enumerate(refs):
        for t in range(9):
            s = group * 9 + t
            value = ref[t * 8 : (t + 1) * 8, :]
            slots[s] = value
            filled = filled + jnp.where(value[7:8, :] > 0.5, 1 << s, 0)
    total = 9 * len(refs)
    slots[total] = jnp.zeros((8, CAP), F32)
    mask = jnp.max(filled)
    count = jnp.int32(0)
    for s in range(total):
        order[count] = s
        count = count + ((mask >> s) & 1)
    order[count] = total
    return count


def pair_block(slots, order, pair):
    return jnp.concatenate([slots[order[2 * pair]], slots[order[2 * pair + 1]]], axis=1)


NT = (((1,), (1,)), ((), ()))
NN = (((1,), (0,)), ((), ()))


def spread(slots, order, count, plane, forcing_ref):
    width = 2 * CAP

    def one_pair(pair, carry):
        block = pair_block(slots, order, pair)
        wx, wy, wz = point_weights(block)
        for i in range(CI):
            high, low = halves(wx[i : i + 1, :] * wy)
            plane[i * CJ : (i + 1) * CJ, :width] = high
            plane[i * CJ : (i + 1) * CJ, width:] = low
        parts = [halves(block[c : c + 1, :] * wz) for c in range(3)]
        both_high = jnp.concatenate([parts[0][0], parts[1][0]], axis=0)
        both_low = jnp.concatenate([parts[0][1], parts[1][1]], axis=0)
        third = jnp.concatenate(parts[2], axis=0)

        def dot(a, b):
            return lax.dot_general(a, b, NT, preferred_element_type=F32)

        step = CI * CJ // SPREAD_PARTS
        for m in range(0, CI * CJ, step):
            high, low = plane[m : m + step, :width], plane[m : m + step, width:]
            pairs = dot(high, both_high) + dot(low, both_high) + dot(high, both_low)
            last = dot(high, third) + dot(low, third)
            for c in range(2):
                first = c * CI * CJ + m
                forcing_ref[first : first + step, :] += pairs[:, c * CK : (c + 1) * CK]
            first = 2 * CI * CJ + m
            forcing_ref[first : first + step, :] += last[:, :CK] + last[:, CK:]
        return carry

    lax.fori_loop(0, (count + 1) // 2, one_pair, 0)


def sample(slots, order, count, field, sampled_ref):
    def one_pair(pair, carry):
        block = pair_block(slots, order, pair)
        wx, wy, wz = point_weights(block)
        high, low = halves(wz)
        high = jnp.concatenate([high, high], axis=0)
        step = CI * CJ // SAMPLE_PARTS
        sums = [jnp.zeros((CJ, 2 * CAP), F32)] * 3
        for m in range(0, CI * CJ, step):
            for c in range(3):
                part = slice(c * CI * CJ + m, c * CI * CJ + m + step)
                along = lax.dot_general(field[part, :], high, NN, preferred_element_type=F32)
                along = along + lax.dot_general(
                    field[part, :CK], low, NN, preferred_element_type=F32
                )
                for t in range(step // CJ):
                    i = m // CJ + t
                    sums[c] = sums[c] + along[t * CJ : (t + 1) * CJ, :] * wx[i : i + 1, :]
        rows = [jnp.sum(sums[c] * wy, axis=0, keepdims=True) for c in range(3)]
        result = jnp.concatenate(rows + [jnp.zeros((5, 2 * CAP), F32)], axis=0)
        sampled_ref[order[2 * pair]] = result[:, :CAP]
        sampled_ref[order[2 * pair + 1]] = result[:, CAP:]
        return carry

    lax.fori_loop(0, (count + 1) // 2, one_pair, 0)


def edge_flags():
    ax, ay, az = (lax.axis_index(n) for n in ("gx", "gy", "gz"))
    nx, ny, nz = (lax.axis_size(n) for n in ("gx", "gy", "gz"))
    return (
        (ax > 0, ax < nx - 1),
        (ay > 0, ay < ny - 1),
        (az > 0, az < nz - 1),
    )


def stage(
    alpha, beta, rows_ref, base_ref, visc_ref, forcing_ref, halos, padded, zsc, out_ref, skip=0
):
    xa, xb, ylo, yhi, zlo, zhi = halos
    even = is_even()
    (x0, x1), (y0, y1), (z0, z1) = edge_flags()
    step_rows = (CI + 4) * PAD_ROWS
    for c in range(3):
        for r in range(2):
            part = slice(skip + (c * 2 + r) * CJ, skip + (c * 2 + r + 1) * CJ)
            lower = jnp.where(even, xb[part, :], xa[part, :])
            upper = jnp.where(even, xa[part, :], xb[part, :])
            for n, (value, ok) in enumerate(((lower, x0), (upper, x1))):
                first = c * step_rows + (n * (CI + 2) + r) * PAD_ROWS + 8
                padded[first : first + CJ, :] = jnp.where(ok, value, 0.0)
        for i in range(0, CI, 8):
            for n, (ref, ok) in enumerate(((ylo, y0), (yhi, y1))):
                for r in range(2):
                    value = ref[r * NS + c * CI + i : r * NS + c * CI + i + 8, :]
                    first = c * step_rows + (i + 2) * PAD_ROWS + (6 + r if n == 0 else 24 + r)
                    padded[pl.ds(first, 8, stride=PAD_ROWS), :] = jnp.where(ok, value, 0.0)
    lane = z_masks()
    low_part = lane % 4 < 2
    for b in range(6):
        part = slice(skip + b * CJ, skip + (b + 1) * CJ)
        zsc[b * CJ : (b + 1) * CJ, :] = jnp.where(
            low_part, jnp.where(z0, zlo[part, :], 0.0), jnp.where(z1, zhi[part, :], 0.0)
        )

    def fill(t, carry):
        for r in range(UNROLL):
            i = t * UNROLL + r
            for c in range(3):
                source = pl.multiple_of((c * CI + i) * CJ, CJ)
                target = pl.multiple_of(c * step_rows + (i + 2) * PAD_ROWS + 8, 8)
                padded[pl.ds(target, CJ), :] = rows_ref[pl.ds(source, CJ), :]
        return carry

    lax.fori_loop(0, CI // UNROLL, fill, 0)

    at0, at01 = lane == 0, lane < 2
    at127, at126 = lane == CK - 1, lane >= CK - 2

    def one_plane(half, u):
        i = half * 32 + u
        visc = (beta * DT) * visc_ref[pl.ds(pl.multiple_of(i * CJ, CJ), CJ), :]
        keep = beta - 6.0 * visc

        def at(c, di, dj):
            first = c * step_rows + (i + 2 + di) * PAD_ROWS + 8 + dj
            return padded[pl.ds(first, CJ), :]

        centre = [at(c, 0, 0) for c in range(3)]
        along = [(beta * DT / 12.0) * value for value in centre]
        for c in range(3):
            here = centre[c]
            block = (2 * c + half) * CJ
            side = pltpu.roll(zsc[block : block + CJ, :], 126 - 4 * u, 1)
            za1 = pltpu.roll(jnp.where(at0, side, here), CK - 1, 1)
            za2 = pltpu.roll(jnp.where(at01, side, here), CK - 2, 1)
            zb1 = pltpu.roll(jnp.where(at127, side, here), 1, 1)
            zb2 = pltpu.roll(jnp.where(at126, side, here), 2, 1)
            xa1, xb1, xa2, xb2 = at(c, 1, 0), at(c, -1, 0), at(c, 2, 0), at(c, -2, 0)
            ya1, yb1, ya2, yb2 = at(c, 0, 1), at(c, 0, -1), at(c, 0, 2), at(c, 0, -2)
            advect = along[0] * (8.0 * (xa1 - xb1) - (xa2 - xb2))
            advect = advect + along[1] * (8.0 * (ya1 - yb1) - (ya2 - yb2))
            advect = advect + along[2] * (8.0 * (za1 - zb1) - (za2 - zb2))
            around = ((xa1 + xb1) + (ya1 + yb1)) + (za1 + zb1)
            where = pl.ds(pl.multiple_of((c * CI + i) * CJ, CJ), CJ)
            fresh = (keep * here + visc * around) - advect + (beta * DT) * forcing_ref[where, :]
            if alpha:
                fresh = fresh + alpha * base_ref[where, :]
            out_ref[where, :] = fresh

    for half in range(2):

        def planes(t, carry, half=half):
            for r in range(UNROLL):
                one_plane(half, t * UNROLL + r)
            return carry

        lax.fori_loop(0, 32 // UNROLL, planes, 0)


def middle_spread_kernel(mid_ref, forcing_ref, slots, order, plane):
    forcing_ref[...] = jnp.zeros_like(forcing_ref)
    spread(slots, order, gather_slots((mid_ref,), slots, order), plane, forcing_ref)


def middle_sample_kernel(mid_ref, field, sampled_ref, slots, order):
    count = gather_slots((mid_ref,), slots, order)
    sampled_ref[...] = jnp.zeros_like(sampled_ref)
    sample(slots, order, count, field, sampled_ref)


def first_kernel(
    zlo, zhi, part_ref, rows_ref, visc_ref, xlo, xhi, ylo, yhi,
    out_ref, forcing_ref, xf_ref, xb_ref, yf_ref, yb_ref, zp_ref,
    slots, order, plane, padded, zsc,
):
    count = gather_slots((zlo, zhi), slots, order)
    forcing_ref[...] = part_ref[...]
    spread(slots, order, count, plane, forcing_ref)
    stage(
        0.0, 1.0, rows_ref, rows_ref, visc_ref, forcing_ref,
        (xlo, xhi, ylo, yhi, zlo, zhi), padded, zsc, out_ref, SLOT_ROWS,
    )
    pack_y(out_ref, yf_ref, yb_ref)
    pack_x(out_ref, xf_ref, xb_ref)
    pack_z(out_ref, zp_ref)


def second_kernel(
    rows_ref, base_ref, visc_ref, forcing_ref, xlo, xhi, ylo, yhi, zlo, zhi,
    out_ref, xf_ref, xb_ref, yf_ref, yb_ref, zp_ref, padded, zsc,
):
    stage(
        0.75, 0.25, rows_ref, base_ref, visc_ref, forcing_ref,
        (xlo, xhi, ylo, yhi, zlo, zhi), padded, zsc, out_ref,
    )
    pack_y(out_ref, yf_ref, yb_ref)
    pack_x(out_ref, xf_ref, xb_ref)
    pack_z(out_ref, zp_ref)


def third_kernel(
    zlo_p, zhi_p, rows_ref, base_ref, visc_ref, forcing_ref, xlo, xhi, ylo, yhi, zlo, zhi,
    out_ref, sampled_ref, field, slots, order, padded, zsc,
):
    stage(
        1.0 / 3.0, 2.0 / 3.0, rows_ref, base_ref, visc_ref, forcing_ref,
        (xlo, xhi, ylo, yhi, zlo, zhi), padded, zsc, out_ref,
    )
    def split(t, carry):
        first = pl.multiple_of(t * 256, 256)
        high, low = halves(out_ref[pl.ds(first, 256), :])
        field[pl.ds(first, 256), :CK] = high
        field[pl.ds(first, 256), CK:] = low
        return carry

    lax.fori_loop(0, NS * CJ // 256, split, 0)
    count = gather_slots((zlo_p, zhi_p), slots, order)
    sampled_ref[...] = jnp.zeros_like(sampled_ref)
    sample(slots, order, count, field, sampled_ref)


def pick_kernel(code_ref, low_ref, mid_ref, high_ref, out_ref):
    picked = [jnp.zeros((3, CAP), F32)] * RUNS
    for group, ref in enumerate((low_ref, mid_ref, high_ref)):
        for t in range(9):
            value = ref[t][:3, :]
            for run in range(RUNS):
                mine = code_ref[run : run + 1, :] == group * 9 + t
                picked[run] = jnp.where(mine, value, picked[run])
    for run in range(RUNS):
        out_ref[:, run * CAP : (run + 1) * CAP] = picked[run]


def exchanged(forward, backward, axis):
    count = lax.axis_size(axis)
    up = [(i, (i + 1) % count) for i in range(count)]
    down = [(target, source) for source, target in up]
    return lax.ppermute(forward, axis, up), lax.ppermute(backward, axis, down)


def swapped(first, second, axis):
    count = lax.axis_size(axis)
    pairs = [[], []]
    for start in range(2):
        for i in range(start, count, 2):
            pairs[start] += [(i, (i + 1) % count), ((i + 1) % count, i)]
    return lax.ppermute(first, axis, pairs[0]), lax.ppermute(second, axis, pairs[1])


def halos_of(xf, xb, yf, yb, zp):
    ylo, yhi = exchanged(yf, yb, "gy")
    xlo, xhi = swapped(xf, xb, "gx")
    zlo, zhi = exchanged(zp, zp, "gz")
    return xlo, xhi, ylo, yhi, zlo, zhi


FACES = (
    shape(6 * CJ, CK), shape(6 * CJ, CK), shape(2 * NS, CK), shape(2 * NS, CK), shape(6 * CJ, CK),
)
STENCIL_SCRATCH = [
    pltpu.VMEM((3 * (CI + 4) * PAD_ROWS, CK), F32),
    pltpu.VMEM((6 * CJ, CK), F32),
]
SLOT_SCRATCH = [pltpu.VMEM((19, 8, CAP), F32), pltpu.SMEM((32,), jnp.int32)]
PLANE = pltpu.VMEM((CI * CJ, 4 * CAP), BF16)


def call(kernel, outs, scratch, *args, in_place=False, cost=None):
    if in_place:
        args = [pltpu.with_memory_space_constraint(a, pltpu.HBM) for a in args]
    return pl.pallas_call(
        kernel,
        out_shape=outs,
        in_specs=[pl.BlockSpec(memory_space=pltpu.HBM) if in_place else vmem()] * len(args),
        out_specs=jax.tree.map(lambda _: vmem(), outs),
        scratch_shapes=scratch,
        compiler_params=params(),
        cost_estimate=cost,
    )(*args)


def per_device(velocity, viscosity, point_force, point_offset, point_cell, point_tile):
    tiles = point_tile.reshape(-1)
    rows = velocity.reshape(NS * CJ, CK)
    visc = viscosity.reshape(CI * CJ, CK)
    cells = point_cell.reshape(RUNS, CAP)

    message = shape(SLOT_ROWS + 6 * CJ, CK)
    mid, codes, xa, xb, yf, yb, zp = call(
        pack_kernel,
        (shape(SLOT_ROWS, CAP), jax.ShapeDtypeStruct((RUNS, CAP), jnp.int32), message, message)
        + FACES[2:],
        [
            pltpu.VMEM((27, 8, CAP), F32),
            pltpu.SMEM((RUNS * CAP,), jnp.int32),
            pltpu.VMEM((3, RUNS * CAP), F32),
            pltpu.VMEM((3, RUNS * CAP), F32),
            pltpu.VMEM((RUNS, CAP), jnp.int32),
            pltpu.VMEM((NS * CJ, CK), F32),
            pltpu.SemaphoreType.DMA((5,)),
        ],
        tiles, point_force, point_offset, cells, rows, in_place=True,
    )

    def slots_of(received):
        return received[:SLOT_ROWS]

    xa, xb = swapped(xa, xb, "gx")
    ylo, yhi = exchanged(yf, yb, "gy")
    held = jnp.stack([slots_of(xa), mid, slots_of(xb)]).reshape(3, 3, 3, 8, CAP)
    from_low, from_high = exchanged(held[:, 2], held[:, 0], "gy")
    held = jnp.stack([from_low, held[:, 1], from_high])
    mine = held[:, :, 1].reshape(SLOT_ROWS, CAP)
    zlo, zhi = exchanged(
        jnp.concatenate([held[:, :, 2].reshape(SLOT_ROWS, CAP), zp]),
        jnp.concatenate([held[:, :, 0].reshape(SLOT_ROWS, CAP), zp]),
        "gz",
    )
    cost = pl.CostEstimate(flops=4_000_000_000, bytes_accessed=4_000_000, transcendentals=200_000)
    part = call(
        middle_spread_kernel, shape(NS * CJ, CK), SLOT_SCRATCH + [PLANE], mine, cost=cost
    )

    section_one, forcing, *faces = call(
        first_kernel, (shape(NS * CJ, CK), shape(NS * CJ, CK)) + FACES,
        SLOT_SCRATCH + [PLANE] + STENCIL_SCRATCH,
        zlo, zhi, part, rows, visc, xa, xb, ylo, yhi,
    )
    section_two, *faces = call(
        second_kernel, (shape(NS * CJ, CK),) + FACES, STENCIL_SCRATCH,
        section_one, rows, visc, forcing, *halos_of(*faces),
    )
    fresh, sampled, field = call(
        third_kernel,
        (
            shape(NS * CJ, CK),
            shape(19, 8, CAP),
            jax.ShapeDtypeStruct((NS * CJ, 2 * CK), BF16),
        ),
        SLOT_SCRATCH + STENCIL_SCRATCH,
        zlo, zhi, section_two, rows, visc, forcing, *halos_of(*faces),
    )

    from_low, from_high = exchanged(sampled[9:18], sampled[:9], "gz")
    middle = call(
        middle_sample_kernel, shape(10, 8, CAP), SLOT_SCRATCH, mine, field, cost=cost
    )
    held = jnp.stack([from_low, middle[:9], from_high]).reshape(3, 3, 3, 8, CAP)
    from_low, from_high = exchanged(held[:, 2], held[:, 0], "gy")
    held = jnp.stack([from_low, held[:, 1], from_high])
    mine = held[:, :, 1].reshape(9, 8, CAP)
    from_first, from_second = swapped(
        held[:, :, 0].reshape(9, 8, CAP), held[:, :, 2].reshape(9, 8, CAP), "gx"
    )
    point_velocity = call(
        pick_kernel, shape(3, RUNS * CAP), [],
        codes, from_first, mine, from_second,
    )
    return fresh.reshape(velocity.shape), point_velocity


def solution(mesh):
    in_specs = (
        P(None, "gx", "gy", "gz"),
        P("gx", "gy", "gz"),
        P(None, ("gx", "gy", "gz")),
        P(None, ("gx", "gy", "gz")),
        P(("gx", "gy", "gz")),
        P(("gx", "gy", "gz"), None),
    )
    out_specs = (P(None, "gx", "gy", "gz"), P(None, ("gx", "gy", "gz")))
    return jax.shard_map(
        per_device, mesh=mesh, in_specs=in_specs, out_specs=out_specs, check_vma=False
    )
```

```python
import jax
import jax.numpy as jnp
from jax import lax
from jax.experimental import pallas as pl
from jax.experimental.pallas import tpu as pltpu
from jax.sharding import PartitionSpec as P


DT = 0.1
CI, CJ, CK = 64, 16, 128
NS = 3 * CI
CAP = 128
RUNS = 8
NY_DEV, NZ_DEV = 4, 4
UNROLL = 4
PACK_UNROLL = 8
SLOT_ROWS = 9 * 8
SPREAD_PARTS = 2
SAMPLE_PARTS = 2
PAD_ROWS = 32
F32 = jnp.float32
BF16 = jnp.bfloat16


def vmem():
    return pl.BlockSpec(memory_space=pltpu.VMEM)


def shape(*dims):
    return jax.ShapeDtypeStruct(dims, F32)


def params():
    return pltpu.CompilerParams(vmem_limit_bytes=40 * 1024 * 1024)


def run_code(tile_ref, run):
    target = tile_ref[run * CAP]
    step_a = target // (NY_DEV * NZ_DEV) - lax.axis_index("gx")
    step_b = (target // NZ_DEV) % NY_DEV - lax.axis_index("gy")
    step_c = target % NZ_DEV - lax.axis_index("gz")
    group = 1 - step_a * (1 - 2 * lax.rem(lax.axis_index("gx"), 2))
    return (group * 3 + step_b + 1) * 3 + step_c + 1


def is_even():
    return lax.rem(lax.axis_index("gx"), 2) == 0


def pack_y(rows_ref, forward_ref, backward_ref):
    for r in range(2):
        for s in range(0, NS, 8):
            forward_ref[r * NS + s : r * NS + s + 8, :] = rows_ref[
                pl.ds(s * CJ + CJ - 2 + r, 8, stride=CJ), :
            ]
            backward_ref[r * NS + s : r * NS + s + 8, :] = rows_ref[
                pl.ds(s * CJ + r, 8, stride=CJ), :
            ]


def pack_x(rows_ref, message_ref, skip=0):
    even = is_even()
    half = skip + 6 * CJ
    for c in range(3):
        base = c * CI * CJ
        upper = rows_ref[base + (CI - 2) * CJ : base + CI * CJ, :]
        lower = rows_ref[base : base + 2 * CJ, :]
        first = skip + c * 2 * CJ
        message_ref[first : first + 2 * CJ, :] = jnp.where(even, upper, lower)
        message_ref[half + first : half + first + 2 * CJ, :] = jnp.where(even, lower, upper)


def z_masks():
    lane = lax.broadcasted_iota(jnp.int32, (CJ, CK), 1)
    return lane


def pack_z(rows_ref, out_ref):
    lane = z_masks()
    group = lane // 4

    def step(t, blocks):
        blocks = list(blocks)
        for r in range(PACK_UNROLL):
            u = t * PACK_UNROLL + r
            for b in range(6):
                first = pl.multiple_of((b * 32 + u) * CJ, CJ)
                turned = pltpu.roll(rows_ref[pl.ds(first, CJ), :], 2 + 4 * u, 1)
                blocks[b] = jnp.where(group == u, turned, blocks[b])
        return tuple(blocks)

    zero = jnp.zeros((CJ, CK), F32)
    blocks = lax.fori_loop(0, 32 // PACK_UNROLL, step, (zero,) * 6)
    for b in range(6):
        out_ref[b * CJ : (b + 1) * CJ, :] = blocks[b]


def pack_kernel(
    tile_any, force_any, offset_any, cell_any, rows_any,
    mid_ref, code_ref, x_ref, yf_ref, yb_ref, zp_ref,
    points_ref, tile_ref, force_ref, offset_ref, cell_ref, rows_ref, sems,
):
    moves = [
        pltpu.make_async_copy(source, target, sems.at[n])
        for n, (source, target) in enumerate(
            (
                (tile_any, tile_ref), (force_any, force_ref), (offset_any, offset_ref),
                (cell_any, cell_ref), (rows_any, rows_ref),
            )
        )
    ]
    for move in moves:
        move.start()
    points_ref[...] = jnp.zeros_like(points_ref)
    for move in moves[:4]:
        move.wait()
    for run in range(RUNS):
        code = run_code(tile_ref, run)
        lanes = slice(run * CAP, (run + 1) * CAP)
        block = jnp.concatenate(
            [
                force_ref[:, lanes],
                offset_ref[:, lanes],
                cell_ref[run : run + 1, :].astype(F32),
                jnp.ones((1, CAP), F32),
            ],
            axis=0,
        )
        points_ref[code] = block
        code_ref[run : run + 1, :] = jnp.full((1, CAP), code, jnp.int32)
    half = SLOT_ROWS + 6 * CJ
    for group, (ref, first) in enumerate(((x_ref, 0), (mid_ref, 0), (x_ref, half))):
        for t in range(9):
            ref[first + t * 8 : first + (t + 1) * 8, :] = points_ref[group * 9 + t]
    moves[4].wait()
    pack_y(rows_ref, yf_ref, yb_ref)
    pack_x(rows_ref, x_ref, SLOT_ROWS)
    pack_z(rows_ref, zp_ref)


def weights_along(centre, count):
    middle = lax.broadcasted_iota(jnp.int32, (count, centre.shape[1]), 0).astype(F32) + 0.5
    scaled = (middle - centre) * 0.5
    raw = jnp.exp(-scaled * scaled)
    return raw * (1.0 / jnp.sum(raw, axis=0, keepdims=True))


def point_weights(block):
    cell = block[6:7, :].astype(jnp.int32)
    first = (cell // (CJ * CK)).astype(F32) + block[3:4, :]
    second = ((cell // CK) % CJ).astype(F32) + block[4:5, :]
    third = (cell % CK).astype(F32) + block[5:6, :]
    return weights_along(first, CI), weights_along(second, CJ), weights_along(third, CK)


def halves(value):
    high = value.astype(BF16)
    return high, (value - high.astype(F32)).astype(BF16)


def gather_slots(refs, slots, order):
    filled = jnp.zeros((1, CAP), jnp.int32)
    for group, ref in enumerate(refs):
        for t in range(9):
            s = group * 9 + t
            value = ref[t * 8 : (t + 1) * 8, :]
            slots[s] = value
            filled = filled + jnp.where(value[7:8, :] > 0.5, 1 << s, 0)
    total = 9 * len(refs)
    slots[total] = jnp.zeros((8, CAP), F32)
    mask = jnp.max(filled)
    count = jnp.int32(0)
    for s in range(total):
        order[count] = s
        count = count + ((mask >> s) & 1)
    order[count] = total
    return count


def pair_block(slots, order, pair):
    return jnp.concatenate([slots[order[2 * pair]], slots[order[2 * pair + 1]]], axis=1)


NT = (((1,), (1,)), ((), ()))
NN = (((1,), (0,)), ((), ()))


def spread(slots, order, count, plane, forcing_ref):
    width = 2 * CAP

    def one_pair(pair, carry):
        block = pair_block(slots, order, pair)
        wx, wy, wz = point_weights(block)
        for i in range(CI):
            high, low = halves(wx[i : i + 1, :] * wy)
            plane[i * CJ : (i + 1) * CJ, :width] = high
            plane[i * CJ : (i + 1) * CJ, width:] = low
        parts = [halves(block[c : c + 1, :] * wz) for c in range(3)]
        both_high = jnp.concatenate([parts[0][0], parts[1][0]], axis=0)
        both_low = jnp.concatenate([parts[0][1], parts[1][1]], axis=0)
        third = jnp.concatenate(parts[2], axis=0)

        def dot(a, b):
            return lax.dot_general(a, b, NT, preferred_element_type=F32)

        step = CI * CJ // SPREAD_PARTS
        for m in range(0, CI * CJ, step):
            high, low = plane[m : m + step, :width], plane[m : m + step, width:]
            pairs = dot(high, both_high) + dot(low, both_high) + dot(high, both_low)
            last = dot(high, third) + dot(low, third)
            for c in range(2):
                first = c * CI * CJ + m
                forcing_ref[first : first + step, :] += pairs[:, c * CK : (c + 1) * CK]
            first = 2 * CI * CJ + m
            forcing_ref[first : first + step, :] += last[:, :CK] + last[:, CK:]
        return carry

    lax.fori_loop(0, (count + 1) // 2, one_pair, 0)


def sample(slots, order, count, field, sampled_ref):
    def one_pair(pair, carry):
        block = pair_block(slots, order, pair)
        wx, wy, wz = point_weights(block)
        high, low = halves(wz)
        high = jnp.concatenate([high, high], axis=0)
        step = CI * CJ // SAMPLE_PARTS
        sums = [jnp.zeros((CJ, 2 * CAP), F32)] * 3
        for m in range(0, CI * CJ, step):
            for c in range(3):
                part = slice(c * CI * CJ + m, c * CI * CJ + m + step)
                along = lax.dot_general(field[part, :], high, NN, preferred_element_type=F32)
                along = along + lax.dot_general(
                    field[part, :CK], low, NN, preferred_element_type=F32
                )
                for t in range(step // CJ):
                    i = m // CJ + t
                    sums[c] = sums[c] + along[t * CJ : (t + 1) * CJ, :] * wx[i : i + 1, :]
        rows = [jnp.sum(sums[c] * wy, axis=0, keepdims=True) for c in range(3)]
        result = jnp.concatenate(rows + [jnp.zeros((5, 2 * CAP), F32)], axis=0)
        sampled_ref[order[2 * pair]] = result[:, :CAP]
        sampled_ref[order[2 * pair + 1]] = result[:, CAP:]
        return carry

    lax.fori_loop(0, (count + 1) // 2, one_pair, 0)


def edge_flags():
    ax, ay, az = (lax.axis_index(n) for n in ("gx", "gy", "gz"))
    nx, ny, nz = (lax.axis_size(n) for n in ("gx", "gy", "gz"))
    return (
        (ax > 0, ax < nx - 1),
        (ay > 0, ay < ny - 1),
        (az > 0, az < nz - 1),
    )


def stage(
    alpha, beta, rows_ref, base_ref, visc_ref, forcing_ref, halos, padded, zsc, out_ref, skip=0
):
    xa, xb, ylo, yhi, zlo, zhi = halos
    even = is_even()
    (x0, x1), (y0, y1), (z0, z1) = edge_flags()
    step_rows = (CI + 4) * PAD_ROWS
    for c in range(3):
        for r in range(2):
            part = slice(skip + (c * 2 + r) * CJ, skip + (c * 2 + r + 1) * CJ)
            lower = jnp.where(even, xb[part, :], xa[part, :])
            upper = jnp.where(even, xa[part, :], xb[part, :])
            for n, (value, ok) in enumerate(((lower, x0), (upper, x1))):
                first = c * step_rows + (n * (CI + 2) + r) * PAD_ROWS + 8
                padded[first : first + CJ, :] = jnp.where(ok, value, 0.0)
        for i in range(0, CI, 8):
            for n, (ref, ok) in enumerate(((ylo, y0), (yhi, y1))):
                for r in range(2):
                    value = ref[r * NS + c * CI + i : r * NS + c * CI + i + 8, :]
                    first = c * step_rows + (i + 2) * PAD_ROWS + (6 + r if n == 0 else 24 + r)
                    padded[pl.ds(first, 8, stride=PAD_ROWS), :] = jnp.where(ok, value, 0.0)
    lane = z_masks()
    low_part = lane % 4 < 2
    for b in range(6):
        part = slice(skip + b * CJ, skip + (b + 1) * CJ)
        zsc[b * CJ : (b + 1) * CJ, :] = jnp.where(
            low_part, jnp.where(z0, zlo[part, :], 0.0), jnp.where(z1, zhi[part, :], 0.0)
        )

    def fill(t, carry):
        for r in range(UNROLL):
            i = t * UNROLL + r
            for c in range(3):
                source = pl.multiple_of((c * CI + i) * CJ, CJ)
                target = pl.multiple_of(c * step_rows + (i + 2) * PAD_ROWS + 8, 8)
                padded[pl.ds(target, CJ), :] = rows_ref[pl.ds(source, CJ), :]
        return carry

    lax.fori_loop(0, CI // UNROLL, fill, 0)

    at0, at01 = lane == 0, lane < 2
    at127, at126 = lane == CK - 1, lane >= CK - 2

    def one_plane(half, u):
        i = half * 32 + u
        visc = (beta * DT) * visc_ref[pl.ds(pl.multiple_of(i * CJ, CJ), CJ), :]
        keep = beta - 6.0 * visc

        def at(c, di, dj):
            first = c * step_rows + (i + 2 + di) * PAD_ROWS + 8 + dj
            return padded[pl.ds(first, CJ), :]

        centre = [at(c, 0, 0) for c in range(3)]
        along = [(beta * DT / 12.0) * value for value in centre]
        for c in range(3):
            here = centre[c]
            block = (2 * c + half) * CJ
            side = pltpu.roll(zsc[block : block + CJ, :], 126 - 4 * u, 1)
            za1 = pltpu.roll(jnp.where(at0, side, here), CK - 1, 1)
            za2 = pltpu.roll(jnp.where(at01, side, here), CK - 2, 1)
            zb1 = pltpu.roll(jnp.where(at127, side, here), 1, 1)
            zb2 = pltpu.roll(jnp.where(at126, side, here), 2, 1)
            xa1, xb1, xa2, xb2 = at(c, 1, 0), at(c, -1, 0), at(c, 2, 0), at(c, -2, 0)
            ya1, yb1, ya2, yb2 = at(c, 0, 1), at(c, 0, -1), at(c, 0, 2), at(c, 0, -2)
            advect = along[0] * (8.0 * (xa1 - xb1) - (xa2 - xb2))
            advect = advect + along[1] * (8.0 * (ya1 - yb1) - (ya2 - yb2))
            advect = advect + along[2] * (8.0 * (za1 - zb1) - (za2 - zb2))
            around = ((xa1 + xb1) + (ya1 + yb1)) + (za1 + zb1)
            where = pl.ds(pl.multiple_of((c * CI + i) * CJ, CJ), CJ)
            fresh = (keep * here + visc * around) - advect + (beta * DT) * forcing_ref[where, :]
            if alpha:
                fresh = fresh + alpha * base_ref[where, :]
            out_ref[where, :] = fresh

    for half in range(2):

        def planes(t, carry, half=half):
            for r in range(UNROLL):
                one_plane(half, t * UNROLL + r)
            return carry

        lax.fori_loop(0, 32 // UNROLL, planes, 0)


def middle_spread_kernel(mid_ref, forcing_ref, slots, order, plane):
    forcing_ref[...] = jnp.zeros_like(forcing_ref)
    spread(slots, order, gather_slots((mid_ref,), slots, order), plane, forcing_ref)


def middle_sample_kernel(mid_ref, field, sampled_ref, slots, order):
    count = gather_slots((mid_ref,), slots, order)
    sampled_ref[...] = jnp.zeros_like(sampled_ref)
    sample(slots, order, count, field, sampled_ref)


def first_kernel(
    zlo, zhi, part_ref, rows_ref, visc_ref, xlo, xhi, ylo, yhi,
    out_ref, forcing_ref, x_ref, yf_ref, yb_ref, zp_ref,
    slots, order, plane, padded, zsc,
):
    count = gather_slots((zlo, zhi), slots, order)
    forcing_ref[...] = part_ref[...]
    spread(slots, order, count, plane, forcing_ref)
    stage(
        0.0, 1.0, rows_ref, rows_ref, visc_ref, forcing_ref,
        (xlo, xhi, ylo, yhi, zlo, zhi), padded, zsc, out_ref, SLOT_ROWS,
    )
    pack_y(out_ref, yf_ref, yb_ref)
    pack_x(out_ref, x_ref)
    pack_z(out_ref, zp_ref)


def second_kernel(
    rows_ref, base_ref, visc_ref, forcing_ref, xlo, xhi, ylo, yhi, zlo, zhi,
    out_ref, x_ref, yf_ref, yb_ref, zp_ref, padded, zsc,
):
    stage(
        0.75, 0.25, rows_ref, base_ref, visc_ref, forcing_ref,
        (xlo, xhi, ylo, yhi, zlo, zhi), padded, zsc, out_ref,
    )
    pack_y(out_ref, yf_ref, yb_ref)
    pack_x(out_ref, x_ref)
    pack_z(out_ref, zp_ref)


def third_kernel(
    zlo_p, zhi_p, rows_ref, base_ref, visc_ref, forcing_ref, xlo, xhi, ylo, yhi, zlo, zhi,
    out_ref, sampled_ref, field, slots, order, padded, zsc,
):
    stage(
        1.0 / 3.0, 2.0 / 3.0, rows_ref, base_ref, visc_ref, forcing_ref,
        (xlo, xhi, ylo, yhi, zlo, zhi), padded, zsc, out_ref,
    )

    def split(t, carry):
        first = pl.multiple_of(t * 256, 256)
        high, low = halves(out_ref[pl.ds(first, 256), :])
        field[pl.ds(first, 256), :CK] = high
        field[pl.ds(first, 256), CK:] = low
        return carry

    lax.fori_loop(0, NS * CJ // 256, split, 0)
    count = gather_slots((zlo_p, zhi_p), slots, order)
    sampled_ref[...] = jnp.zeros_like(sampled_ref)
    sample(slots, order, count, field, sampled_ref)


def pick_kernel(code_ref, low_ref, mid_ref, high_ref, out_ref):
    picked = [jnp.zeros((3, CAP), F32)] * RUNS
    for group, ref in enumerate((low_ref, mid_ref, high_ref)):
        for t in range(9):
            value = ref[t][:3, :]
            for run in range(RUNS):
                mine = code_ref[run : run + 1, :] == group * 9 + t
                picked[run] = jnp.where(mine, value, picked[run])
    for run in range(RUNS):
        out_ref[:, run * CAP : (run + 1) * CAP] = picked[run]


def exchanged(forward, backward, axis):
    count = lax.axis_size(axis)
    up = [(i, (i + 1) % count) for i in range(count)]
    down = [(target, source) for source, target in up]
    low = lax.ppermute(forward, axis, up)
    high = lax.ppermute(backward, axis, down)
    return low, high


def swapped(first, second, axis):
    count = lax.axis_size(axis)
    pairs = [[], []]
    for start in range(2):
        for i in range(start, count, 2):
            pairs[start] += [(i, (i + 1) % count), ((i + 1) % count, i)]
    return lax.ppermute(first, axis, pairs[0]), lax.ppermute(second, axis, pairs[1])


def passed_on(message, axis):
    count = lax.axis_size(axis)
    across = [(i, i + 1 - 2 * (i % 2)) for i in range(count)]
    onward = [(i, (i + 2 - 4 * (i % 2)) % count) for i in range(count)]
    near = lax.ppermute(message, axis, across)
    return near, lax.ppermute(near[message.shape[0] // 2 :], axis, onward)


def halos_of(x, yf, yb, zp):
    xlo, xhi = passed_on(x, "gx")
    ylo, yhi = exchanged(yf, yb, "gy")
    zlo, zhi = exchanged(zp, zp, "gz")
    return xlo, xhi, ylo, yhi, zlo, zhi


FACES = (
    shape(12 * CJ, CK), shape(2 * NS, CK), shape(2 * NS, CK), shape(6 * CJ, CK),
)
STENCIL_SCRATCH = [
    pltpu.VMEM((3 * (CI + 4) * PAD_ROWS, CK), F32),
    pltpu.VMEM((6 * CJ, CK), F32),
]
SLOT_SCRATCH = [pltpu.VMEM((19, 8, CAP), F32), pltpu.SMEM((32,), jnp.int32)]
PLANE = pltpu.VMEM((CI * CJ, 4 * CAP), BF16)


def call(kernel, outs, scratch, *args, in_place=False, cost=None):
    if in_place:
        args = [pltpu.with_memory_space_constraint(a, pltpu.HBM) for a in args]
    return pl.pallas_call(
        kernel,
        out_shape=outs,
        in_specs=[pl.BlockSpec(memory_space=pltpu.HBM) if in_place else vmem()] * len(args),
        out_specs=jax.tree.map(lambda _: vmem(), outs),
        scratch_shapes=scratch,
        compiler_params=params(),
        cost_estimate=cost,
    )(*args)


def per_device(velocity, viscosity, point_force, point_offset, point_cell, point_tile):
    tiles = point_tile.reshape(-1)
    rows = velocity.reshape(NS * CJ, CK)
    visc = viscosity.reshape(CI * CJ, CK)
    cells = point_cell.reshape(RUNS, CAP)

    message = shape(2 * (SLOT_ROWS + 6 * CJ), CK)
    mid, codes, x, yf, yb, zp = call(
        pack_kernel,
        (shape(SLOT_ROWS, CAP), jax.ShapeDtypeStruct((RUNS, CAP), jnp.int32), message)
        + FACES[1:],
        [
            pltpu.VMEM((27, 8, CAP), F32),
            pltpu.SMEM((RUNS * CAP,), jnp.int32),
            pltpu.VMEM((3, RUNS * CAP), F32),
            pltpu.VMEM((3, RUNS * CAP), F32),
            pltpu.VMEM((RUNS, CAP), jnp.int32),
            pltpu.VMEM((NS * CJ, CK), F32),
            pltpu.SemaphoreType.DMA((5,)),
        ],
        tiles, point_force, point_offset, cells, rows, in_place=True,
    )

    def slots_of(received):
        return received[:SLOT_ROWS]

    xa, xb = passed_on(x, "gx")
    ylo, yhi = exchanged(yf, yb, "gy")
    far = slots_of(xb)
    held = jnp.stack([slots_of(xa), mid, far]).reshape(3, 3, 3, 8, CAP)
    from_low, from_high = exchanged(held[:, 2], held[:, 0], "gy")
    held = jnp.stack([from_low, held[:, 1], from_high])
    mine = held[:, :, 1].reshape(SLOT_ROWS, CAP)
    zlo, zhi = exchanged(
        jnp.concatenate([held[:, :, 2].reshape(SLOT_ROWS, CAP), zp]),
        jnp.concatenate([held[:, :, 0].reshape(SLOT_ROWS, CAP), zp]),
        "gz",
    )
    cost = pl.CostEstimate(flops=4_000_000_000, bytes_accessed=4_000_000, transcendentals=200_000)
    part = call(
        middle_spread_kernel, shape(NS * CJ, CK), SLOT_SCRATCH + [PLANE], mine, cost=cost
    )

    section_one, forcing, *faces = call(
        first_kernel, (shape(NS * CJ, CK), shape(NS * CJ, CK)) + FACES,
        SLOT_SCRATCH + [PLANE] + STENCIL_SCRATCH,
        zlo, zhi, part, rows, visc, xa, xb, ylo, yhi,
    )
    section_two, *faces = call(
        second_kernel, (shape(NS * CJ, CK),) + FACES, STENCIL_SCRATCH,
        section_one, rows, visc, forcing, *halos_of(*faces),
    )
    fresh, sampled, field = call(
        third_kernel,
        (
            shape(NS * CJ, CK),
            shape(19, 8, CAP),
            jax.ShapeDtypeStruct((NS * CJ, 2 * CK), BF16),
        ),
        SLOT_SCRATCH + STENCIL_SCRATCH,
        zlo, zhi, section_two, rows, visc, forcing, *halos_of(*faces),
    )

    from_low, from_high = exchanged(sampled[9:18], sampled[:9], "gz")
    middle = call(
        middle_sample_kernel, shape(10, 8, CAP), SLOT_SCRATCH, mine, field, cost=cost
    )
    held = jnp.stack([from_low, middle[:9], from_high]).reshape(3, 3, 3, 8, CAP)
    from_low, from_high = exchanged(held[:, 2], held[:, 0], "gy")
    held = jnp.stack([from_low, held[:, 1], from_high])
    mine = held[:, :, 1].reshape(9, 8, CAP)
    from_first, from_second = swapped(
        held[:, :, 0].reshape(9, 8, CAP), held[:, :, 2].reshape(9, 8, CAP), "gx"
    )
    point_velocity = call(
        pick_kernel, shape(3, RUNS * CAP), [],
        codes, from_first, mine, from_second,
    )
    return fresh.reshape(velocity.shape), point_velocity


def solution(mesh):
    in_specs = (
        P(None, "gx", "gy", "gz"),
        P("gx", "gy", "gz"),
        P(None, ("gx", "gy", "gz")),
        P(None, ("gx", "gy", "gz")),
        P(("gx", "gy", "gz")),
        P(("gx", "gy", "gz"), None),
    )
    out_specs = (P(None, "gx", "gy", "gz"), P(None, ("gx", "gy", "gz")))

    return jax.shard_map(per_device, mesh=mesh, in_specs=in_specs, out_specs=out_specs, check_vma=False)
```

```python
import functools

import jax
import jax.numpy as jnp
from jax import lax
from jax.experimental import pallas as pl
from jax.experimental.pallas import tpu as pltpu
from jax.sharding import PartitionSpec as P


DT = 0.1
CI, CJ, CK = 64, 16, 128
NS = 3 * CI
CAP = 128
RUNS = 8
NY_DEV, NZ_DEV = 4, 4
UNROLL = 4
PACK_UNROLL = 8
SLOT_ROWS = 9 * 8
SPREAD_PARTS = 2
SAMPLE_PARTS = 2
PAD_ROWS = 32
F32 = jnp.float32
BF16 = jnp.bfloat16


def vmem():
    return pl.BlockSpec(memory_space=pltpu.VMEM)


def shape(*dims):
    return jax.ShapeDtypeStruct(dims, F32)


def params():
    return pltpu.CompilerParams(vmem_limit_bytes=40 * 1024 * 1024)


def run_code(tile_ref, run):
    target = tile_ref[run * CAP]
    step_a = target // (NY_DEV * NZ_DEV) - lax.axis_index("gx")
    step_b = (target // NZ_DEV) % NY_DEV - lax.axis_index("gy")
    step_c = target % NZ_DEV - lax.axis_index("gz")
    group = 1 - step_a * (1 - 2 * lax.rem(lax.axis_index("gx"), 2))
    return (group * 3 + step_b + 1) * 3 + step_c + 1


def is_even():
    return lax.rem(lax.axis_index("gx"), 2) == 0


def pack_y(rows_ref, forward_ref, backward_ref):
    for r in range(2):
        for s in range(0, NS, 8):
            forward_ref[r * NS + s : r * NS + s + 8, :] = rows_ref[
                pl.ds(s * CJ + CJ - 2 + r, 8, stride=CJ), :
            ]
            backward_ref[r * NS + s : r * NS + s + 8, :] = rows_ref[
                pl.ds(s * CJ + r, 8, stride=CJ), :
            ]


def pack_x(rows_ref, first_ref, second_ref, skip=0):
    even = is_even()
    for c in range(3):
        base = c * CI * CJ
        upper = rows_ref[base + (CI - 2) * CJ : base + CI * CJ, :]
        lower = rows_ref[base : base + 2 * CJ, :]
        part = slice(skip + c * 2 * CJ, skip + (c + 1) * 2 * CJ)
        first_ref[part, :] = jnp.where(even, upper, lower)
        second_ref[part, :] = jnp.where(even, lower, upper)


def z_masks():
    lane = lax.broadcasted_iota(jnp.int32, (CJ, CK), 1)
    return lane


def pack_z(rows_ref, out_ref):
    lane = z_masks()
    group = lane // 4

    def step(t, blocks):
        blocks = list(blocks)
        for r in range(PACK_UNROLL):
            u = t * PACK_UNROLL + r
            for b in range(6):
                first = pl.multiple_of((b * 32 + u) * CJ, CJ)
                turned = pltpu.roll(rows_ref[pl.ds(first, CJ), :], 2 + 4 * u, 1)
                blocks[b] = jnp.where(group == u, turned, blocks[b])
        return tuple(blocks)

    zero = jnp.zeros((CJ, CK), F32)
    blocks = lax.fori_loop(0, 32 // PACK_UNROLL, step, (zero,) * 6)
    for b in range(6):
        out_ref[b * CJ : (b + 1) * CJ, :] = blocks[b]


def pack_kernel(
    tile_any, force_any, offset_any, cell_any, rows_any,
    mid_ref, code_ref, xa_ref, xb_ref, yf_ref, yb_ref, zp_ref,
    points_ref, tile_ref, force_ref, offset_ref, cell_ref, rows_ref, sems,
):
    moves = [
        pltpu.make_async_copy(source, target, sems.at[n])
        for n, (source, target) in enumerate(
            (
                (tile_any, tile_ref), (force_any, force_ref), (offset_any, offset_ref),
                (cell_any, cell_ref), (rows_any, rows_ref),
            )
        )
    ]
    for move in moves:
        move.start()
    points_ref[...] = jnp.zeros_like(points_ref)
    for move in moves[:4]:
        move.wait()
    for run in range(RUNS):
        code = run_code(tile_ref, run)
        lanes = slice(run * CAP, (run + 1) * CAP)
        block = jnp.concatenate(
            [
                force_ref[:, lanes],
                offset_ref[:, lanes],
                cell_ref[run : run + 1, :].astype(F32),
                jnp.ones((1, CAP), F32),
            ],
            axis=0,
        )
        points_ref[code] = block
        code_ref[run : run + 1, :] = jnp.full((1, CAP), code, jnp.int32)
    for group, ref in enumerate((xa_ref, mid_ref, xb_ref)):
        for t in range(9):
            ref[t * 8 : (t + 1) * 8, :] = points_ref[group * 9 + t]
    moves[4].wait()
    pack_y(rows_ref, yf_ref, yb_ref)
    pack_x(rows_ref, xa_ref, xb_ref, SLOT_ROWS)
    pack_z(rows_ref, zp_ref)


def weights_along(centre, count):
    middle = lax.broadcasted_iota(jnp.int32, (count, centre.shape[1]), 0).astype(F32) + 0.5
    scaled = (middle - centre) * 0.5
    raw = jnp.exp(-scaled * scaled)
    return raw * (1.0 / jnp.sum(raw, axis=0, keepdims=True))


def point_weights(block):
    cell = block[6:7, :].astype(jnp.int32)
    first = (cell // (CJ * CK)).astype(F32) + block[3:4, :]
    second = ((cell // CK) % CJ).astype(F32) + block[4:5, :]
    third = (cell % CK).astype(F32) + block[5:6, :]
    return weights_along(first, CI), weights_along(second, CJ), weights_along(third, CK)


def halves(value):
    high = value.astype(BF16)
    return high, (value - high.astype(F32)).astype(BF16)


def gather_slots(refs, slots, order, picks=tuple(range(9))):
    filled = jnp.zeros((1, CAP), jnp.int32)
    for group, ref in enumerate(refs):
        for n, t in enumerate(picks):
            s = group * len(picks) + n
            value = ref[t * 8 : (t + 1) * 8, :]
            slots[s] = value
            filled = filled + jnp.where(value[7:8, :] > 0.5, 1 << s, 0)
    total = len(picks) * len(refs)
    slots[total] = jnp.zeros((8, CAP), F32)
    mask = jnp.max(filled)
    count = jnp.int32(0)
    for s in range(total):
        order[count] = s
        count = count + ((mask >> s) & 1)
    order[count] = total
    return count


def pair_block(slots, order, pair):
    return jnp.concatenate([slots[order[2 * pair]], slots[order[2 * pair + 1]]], axis=1)


NT = (((1,), (1,)), ((), ()))
NN = (((1,), (0,)), ((), ()))


def spread(slots, order, count, plane, forcing_ref):
    width = 2 * CAP

    def one_pair(pair, carry):
        block = pair_block(slots, order, pair)
        wx, wy, wz = point_weights(block)
        for i in range(CI):
            high, low = halves(wx[i : i + 1, :] * wy)
            plane[i * CJ : (i + 1) * CJ, :width] = high
            plane[i * CJ : (i + 1) * CJ, width:] = low
        parts = [halves(block[c : c + 1, :] * wz) for c in range(3)]
        both_high = jnp.concatenate([parts[0][0], parts[1][0]], axis=0)
        both_low = jnp.concatenate([parts[0][1], parts[1][1]], axis=0)
        third = jnp.concatenate(parts[2], axis=0)

        def dot(a, b):
            return lax.dot_general(a, b, NT, preferred_element_type=F32)

        step = CI * CJ // SPREAD_PARTS
        for m in range(0, CI * CJ, step):
            high, low = plane[m : m + step, :width], plane[m : m + step, width:]
            pairs = dot(high, both_high) + dot(low, both_high) + dot(high, both_low)
            last = dot(high, third) + dot(low, third)
            for c in range(2):
                first = c * CI * CJ + m
                forcing_ref[first : first + step, :] += pairs[:, c * CK : (c + 1) * CK]
            first = 2 * CI * CJ + m
            forcing_ref[first : first + step, :] += last[:, :CK] + last[:, CK:]
        return carry

    lax.fori_loop(0, (count + 1) // 2, one_pair, 0)


def sample(slots, order, count, field, sampled_ref):
    def one_pair(pair, carry):
        block = pair_block(slots, order, pair)
        wx, wy, wz = point_weights(block)
        high, low = halves(wz)
        high = jnp.concatenate([high, high], axis=0)
        step = CI * CJ // SAMPLE_PARTS
        sums = [jnp.zeros((CJ, 2 * CAP), F32)] * 3
        for m in range(0, CI * CJ, step):
            for c in range(3):
                part = slice(c * CI * CJ + m, c * CI * CJ + m + step)
                along = lax.dot_general(field[part, :], high, NN, preferred_element_type=F32)
                along = along + lax.dot_general(
                    field[part, :CK], low, NN, preferred_element_type=F32
                )
                for t in range(step // CJ):
                    i = m // CJ + t
                    sums[c] = sums[c] + along[t * CJ : (t + 1) * CJ, :] * wx[i : i + 1, :]
        rows = [jnp.sum(sums[c] * wy, axis=0, keepdims=True) for c in range(3)]
        result = jnp.concatenate(rows + [jnp.zeros((5, 2 * CAP), F32)], axis=0)
        sampled_ref[order[2 * pair]] = result[:, :CAP]
        sampled_ref[order[2 * pair + 1]] = result[:, CAP:]
        return carry

    lax.fori_loop(0, (count + 1) // 2, one_pair, 0)


def edge_flags():
    ax, ay, az = (lax.axis_index(n) for n in ("gx", "gy", "gz"))
    nx, ny, nz = (lax.axis_size(n) for n in ("gx", "gy", "gz"))
    return (
        (ax > 0, ax < nx - 1),
        (ay > 0, ay < ny - 1),
        (az > 0, az < nz - 1),
    )


def stage(
    alpha, beta, rows_ref, base_ref, visc_ref, forcing_ref, halos, padded, zsc, out_ref, skip=0
):
    xa, xb, ylo, yhi, zlo, zhi = halos
    even = is_even()
    (x0, x1), (y0, y1), (z0, z1) = edge_flags()
    step_rows = (CI + 4) * PAD_ROWS
    for c in range(3):
        for r in range(2):
            part = slice(skip + (c * 2 + r) * CJ, skip + (c * 2 + r + 1) * CJ)
            lower = jnp.where(even, xb[part, :], xa[part, :])
            upper = jnp.where(even, xa[part, :], xb[part, :])
            for n, (value, ok) in enumerate(((lower, x0), (upper, x1))):
                first = c * step_rows + (n * (CI + 2) + r) * PAD_ROWS + 8
                padded[first : first + CJ, :] = jnp.where(ok, value, 0.0)
        for i in range(0, CI, 8):
            for n, (ref, ok) in enumerate(((ylo, y0), (yhi, y1))):
                for r in range(2):
                    value = ref[r * NS + c * CI + i : r * NS + c * CI + i + 8, :]
                    first = c * step_rows + (i + 2) * PAD_ROWS + (6 + r if n == 0 else 24 + r)
                    padded[pl.ds(first, 8, stride=PAD_ROWS), :] = jnp.where(ok, value, 0.0)
    lane = z_masks()
    low_part = lane % 4 < 2
    for b in range(6):
        part = slice(skip + b * CJ, skip + (b + 1) * CJ)
        zsc[b * CJ : (b + 1) * CJ, :] = jnp.where(
            low_part, jnp.where(z0, zlo[part, :], 0.0), jnp.where(z1, zhi[part, :], 0.0)
        )

    def fill(t, carry):
        for r in range(UNROLL):
            i = t * UNROLL + r
            for c in range(3):
                source = pl.multiple_of((c * CI + i) * CJ, CJ)
                target = pl.multiple_of(c * step_rows + (i + 2) * PAD_ROWS + 8, 8)
                padded[pl.ds(target, CJ), :] = rows_ref[pl.ds(source, CJ), :]
        return carry

    lax.fori_loop(0, CI // UNROLL, fill, 0)

    at0, at01 = lane == 0, lane < 2
    at127, at126 = lane == CK - 1, lane >= CK - 2

    def one_plane(half, u):
        i = half * 32 + u
        visc = (beta * DT) * visc_ref[pl.ds(pl.multiple_of(i * CJ, CJ), CJ), :]
        keep = beta - 6.0 * visc

        def at(c, di, dj):
            first = c * step_rows + (i + 2 + di) * PAD_ROWS + 8 + dj
            return padded[pl.ds(first, CJ), :]

        centre = [at(c, 0, 0) for c in range(3)]
        along = [(beta * DT / 12.0) * value for value in centre]
        for c in range(3):
            here = centre[c]
            block = (2 * c + half) * CJ
            side = pltpu.roll(zsc[block : block + CJ, :], 126 - 4 * u, 1)
            za1 = pltpu.roll(jnp.where(at0, side, here), CK - 1, 1)
            za2 = pltpu.roll(jnp.where(at01, side, here), CK - 2, 1)
            zb1 = pltpu.roll(jnp.where(at127, side, here), 1, 1)
            zb2 = pltpu.roll(jnp.where(at126, side, here), 2, 1)
            xa1, xb1, xa2, xb2 = at(c, 1, 0), at(c, -1, 0), at(c, 2, 0), at(c, -2, 0)
            ya1, yb1, ya2, yb2 = at(c, 0, 1), at(c, 0, -1), at(c, 0, 2), at(c, 0, -2)
            advect = along[0] * (8.0 * (xa1 - xb1) - (xa2 - xb2))
            advect = advect + along[1] * (8.0 * (ya1 - yb1) - (ya2 - yb2))
            advect = advect + along[2] * (8.0 * (za1 - zb1) - (za2 - zb2))
            around = ((xa1 + xb1) + (ya1 + yb1)) + (za1 + zb1)
            where = pl.ds(pl.multiple_of((c * CI + i) * CJ, CJ), CJ)
            fresh = (keep * here + visc * around) - advect + (beta * DT) * forcing_ref[where, :]
            if alpha:
                fresh = fresh + alpha * base_ref[where, :]
            out_ref[where, :] = fresh

    for half in range(2):

        def planes(t, carry, half=half):
            for r in range(UNROLL):
                one_plane(half, t * UNROLL + r)
            return carry

        lax.fori_loop(0, 32 // UNROLL, planes, 0)


def middle_spread_kernel(mid_ref, forcing_ref, slots, order, plane):
    forcing_ref[...] = jnp.zeros_like(forcing_ref)
    spread(slots, order, gather_slots((mid_ref,), slots, order), plane, forcing_ref)


def middle_sample_kernel(picks, mid_ref, field, sampled_ref, slots, order):
    count = gather_slots((mid_ref,), slots, order, picks)
    sampled_ref[...] = jnp.zeros_like(sampled_ref)
    sample(slots, order, count, field, sampled_ref)


def first_kernel(
    zlo, zhi, part_ref, rows_ref, visc_ref, xlo, xhi, ylo, yhi,
    out_ref, forcing_ref, xf_ref, xb_ref, yf_ref, yb_ref, zp_ref,
    slots, order, plane, padded, zsc,
):
    count = gather_slots((zlo, zhi), slots, order)
    forcing_ref[...] = part_ref[...]
    spread(slots, order, count, plane, forcing_ref)
    stage(
        0.0, 1.0, rows_ref, rows_ref, visc_ref, forcing_ref,
        (xlo, xhi, ylo, yhi, zlo, zhi), padded, zsc, out_ref, SLOT_ROWS,
    )
    pack_y(out_ref, yf_ref, yb_ref)
    pack_x(out_ref, xf_ref, xb_ref)
    pack_z(out_ref, zp_ref)


def second_kernel(
    rows_ref, base_ref, visc_ref, forcing_ref, xlo, xhi, ylo, yhi, zlo, zhi,
    out_ref, xf_ref, xb_ref, yf_ref, yb_ref, zp_ref, padded, zsc,
):
    stage(
        0.75, 0.25, rows_ref, base_ref, visc_ref, forcing_ref,
        (xlo, xhi, ylo, yhi, zlo, zhi), padded, zsc, out_ref,
    )
    pack_y(out_ref, yf_ref, yb_ref)
    pack_x(out_ref, xf_ref, xb_ref)
    pack_z(out_ref, zp_ref)


def third_kernel(
    zlo_p, zhi_p, rows_ref, base_ref, visc_ref, forcing_ref, xlo, xhi, ylo, yhi, zlo, zhi,
    out_ref, sampled_ref, field, slots, order, padded, zsc,
):
    stage(
        1.0 / 3.0, 2.0 / 3.0, rows_ref, base_ref, visc_ref, forcing_ref,
        (xlo, xhi, ylo, yhi, zlo, zhi), padded, zsc, out_ref,
    )

    def split(t, carry):
        first = pl.multiple_of(t * 256, 256)
        high, low = halves(out_ref[pl.ds(first, 256), :])
        field[pl.ds(first, 256), :CK] = high
        field[pl.ds(first, 256), CK:] = low
        return carry

    lax.fori_loop(0, NS * CJ // 256, split, 0)
    count = gather_slots((zlo_p, zhi_p), slots, order)
    sampled_ref[...] = jnp.zeros_like(sampled_ref)
    sample(slots, order, count, field, sampled_ref)


def pick_kernel(code_ref, low_ref, mid_ref, high_ref, out_ref):
    picked = [jnp.zeros((3, CAP), F32)] * RUNS
    for group, ref in enumerate((low_ref, mid_ref, high_ref)):
        for t in range(9):
            value = ref[t][:3, :]
            for run in range(RUNS):
                mine = code_ref[run : run + 1, :] == group * 9 + t
                picked[run] = jnp.where(mine, value, picked[run])
    for run in range(RUNS):
        out_ref[:, run * CAP : (run + 1) * CAP] = picked[run]


def exchanged(forward, backward, axis):
    count = lax.axis_size(axis)
    up = [(i, (i + 1) % count) for i in range(count)]
    down = [(target, source) for source, target in up]
    low = lax.ppermute(forward, axis, up)
    high = lax.ppermute(backward, axis, down)
    return low, high


def swapped(first, second, axis):
    count = lax.axis_size(axis)
    pairs = [[], []]
    for start in range(2):
        for i in range(start, count, 2):
            pairs[start] += [(i, (i + 1) % count), ((i + 1) % count, i)]
    return lax.ppermute(first, axis, pairs[0]), lax.ppermute(second, axis, pairs[1])


def halos_of(xf, xb, yf, yb, zp):
    ylo, yhi = exchanged(yf, yb, "gy")
    xlo, xhi = swapped(xf, xb, "gx")
    zlo, zhi = exchanged(zp, zp, "gz")
    return xlo, xhi, ylo, yhi, zlo, zhi


FACES = (
    shape(6 * CJ, CK), shape(6 * CJ, CK), shape(2 * NS, CK), shape(2 * NS, CK), shape(6 * CJ, CK),
)
STENCIL_SCRATCH = [
    pltpu.VMEM((3 * (CI + 4) * PAD_ROWS, CK), F32),
    pltpu.VMEM((6 * CJ, CK), F32),
]
SLOT_SCRATCH = [pltpu.VMEM((19, 8, CAP), F32), pltpu.SMEM((32,), jnp.int32)]
PLANE = pltpu.VMEM((CI * CJ, 4 * CAP), BF16)


def call(kernel, outs, scratch, *args, in_place=False, cost=None):
    if in_place:
        args = [pltpu.with_memory_space_constraint(a, pltpu.HBM) for a in args]
    return pl.pallas_call(
        kernel,
        out_shape=outs,
        in_specs=[pl.BlockSpec(memory_space=pltpu.HBM) if in_place else vmem()] * len(args),
        out_specs=jax.tree.map(lambda _: vmem(), outs),
        scratch_shapes=scratch,
        compiler_params=params(),
        cost_estimate=cost,
    )(*args)


def per_device(velocity, viscosity, point_force, point_offset, point_cell, point_tile):
    tiles = point_tile.reshape(-1)
    rows = velocity.reshape(NS * CJ, CK)
    visc = viscosity.reshape(CI * CJ, CK)
    cells = point_cell.reshape(RUNS, CAP)

    message = shape(SLOT_ROWS + 6 * CJ, CK)
    mid, codes, xa, xb, yf, yb, zp = call(
        pack_kernel,
        (shape(SLOT_ROWS, CAP), jax.ShapeDtypeStruct((RUNS, CAP), jnp.int32), message, message)
        + FACES[2:],
        [
            pltpu.VMEM((27, 8, CAP), F32),
            pltpu.SMEM((RUNS * CAP,), jnp.int32),
            pltpu.VMEM((3, RUNS * CAP), F32),
            pltpu.VMEM((3, RUNS * CAP), F32),
            pltpu.VMEM((RUNS, CAP), jnp.int32),
            pltpu.VMEM((NS * CJ, CK), F32),
            pltpu.SemaphoreType.DMA((5,)),
        ],
        tiles, point_force, point_offset, cells, rows, in_place=True,
    )

    def slots_of(received):
        return received[:SLOT_ROWS]

    xa, xb = swapped(xa, xb, "gx")
    ylo, yhi = exchanged(yf, yb, "gy")
    held = jnp.stack([slots_of(xa), mid, slots_of(xb)]).reshape(3, 3, 3, 8, CAP)
    from_low, from_high = exchanged(held[:, 2], held[:, 0], "gy")
    held = jnp.stack([from_low, held[:, 1], from_high])
    mine = held[:, :, 1].reshape(SLOT_ROWS, CAP)
    zlo, zhi = exchanged(
      jnp.concatenate([held[:, :, 2].reshape(SLOT_ROWS, CAP), zp]),
      jnp.concatenate([held[:, :, 0].reshape(SLOT_ROWS, CAP), zp]),
      "gz",
    )
    cost = pl.CostEstimate(flops=4_000_000_000, bytes_accessed=4_000_000, transcendentals=200_000)
    part = call(
      middle_spread_kernel, shape(NS * CJ, CK), SLOT_SCRATCH + [PLANE], mine, cost=cost
    )

    section_one, forcing, *faces = call(
        first_kernel, (shape(NS * CJ, CK), shape(NS * CJ, CK)) + FACES,
        SLOT_SCRATCH + [PLANE] + STENCIL_SCRATCH,
        zlo, zhi, part, rows, visc, xa, xb, ylo, yhi,
    )
    section_two, *faces = call(
        second_kernel, (shape(NS * CJ, CK),) + FACES, STENCIL_SCRATCH,
        section_one, rows, visc, forcing, *halos_of(*faces),
    )
    fresh, sampled, field = call(
        third_kernel,
        (
            shape(NS * CJ, CK),
            shape(19, 8, CAP),
            jax.ShapeDtypeStruct((NS * CJ, 2 * CK), BF16),
        ),
        SLOT_SCRATCH + STENCIL_SCRATCH,
        zlo, zhi, section_two, rows, visc, forcing, *halos_of(*faces),
    )

    def middle(picks, blocks):
        return call(
            functools.partial(middle_sample_kernel, picks),
            shape(len(picks) + 1, 8, CAP), SLOT_SCRATCH, blocks, field, cost=cost,
        )

    outer = middle((0, 1, 2, 6, 7, 8), mine)
    low, high = exchanged(sampled[9:18], sampled[:9], "gz")
    low, high, after = lax.optimization_barrier((low, high, mine))
    up, down = (jnp.stack([low[t : t + 3], outer[n : n + 3], high[t : t + 3]]) for t, n in ((6, 3), (0, 0)))
    from_low, from_high = exchanged(up, down, "gy")
    inner = middle((3, 4, 5), after)
    centre = jnp.stack([low[3:6], inner[:3], high[3:6]])
    held = jnp.stack([from_low, centre, from_high])
    mine = held[:, :, 1].reshape(9, 8, CAP)
    from_first, from_second = swapped(
        held[:, :, 0].reshape(9, 8, CAP), held[:, :, 2].reshape(9, 8, CAP), "gx"
    )
    point_velocity = call(
        pick_kernel, shape(3, RUNS * CAP), [],
        codes, from_first, mine, from_second,
    )
    return fresh.reshape(velocity.shape), point_velocity


def solution(mesh):
    in_specs = (
        P(None, "gx", "gy", "gz"),
        P("gx", "gy", "gz"),
        P(None, ("gx", "gy", "gz")),
        P(None, ("gx", "gy", "gz")),
        P(("gx", "gy", "gz")),
        P(("gx", "gy", "gz"), None),
    )
    out_specs = (P(None, "gx", "gy", "gz"), P(None, ("gx", "gy", "gz")))

    return jax.shard_map(per_device, mesh=mesh, in_specs=in_specs, out_specs=out_specs, check_vma=False)
```
